256 devices in a mesh: pole: 4 (over y), row: 8 (over z), col: 8 (over x, core).
Axes of the slice: x: 4, y: 4, z: 8, core: 2. Of those that a mesh axis runs over, the one named last changes fastest.
Arguments:
- root_inverse: float32 [8, 1024, 1024], P('pole', ('row', 'col')), may hold values from -100 to 100
- node_factor: float32 [8, 8, 1024, 512], P('pole', 'row', None, 'col'), may hold values from -0.1875 to 0.1875
- node_inverse: float32 [8, 8, 512, 512], P('pole', 'row'), may hold values from -100 to 100
- leaf_root_factor: float32 [8, 64, 1024, 256], P('pole', ('row', 'col')), may hold values from -0.1875 to 0.1875
- leaf_node_factor: float32 [8, 64, 512, 256], P('pole', ('row', 'col')), may hold values from -0.25 to 0.25
- leaf_inverse: float32 [8, 64, 256, 256], P('pole', ('row', 'col')), may hold values from -100 to 100
- leaf_pattern: int32 [64, 8], P(('row', 'col')), may hold values 0 or 1
- pole_weight: float32 [8], P('pole'), may hold values from 0.1 to 1
Outputs:
- root_block: float32 [1024, 1024], P(('row', 'col'))
- node_offdiag: float32 [8, 1024, 512], P('row', None, 'col')
- node_diag: float32 [8, 512, 512], P('row', 'col')
- leaf_root: float32 [64, 1024, 256], P(('row', 'col'))
- leaf_node: float32 [64, 512, 256], P(('row', 'col'))
- leaf_diag: float32 [64, 256, 256], P(('row', 'col'))
The draws below stay inside these ranges and needn't reach their ends.
All inputs are finite; a program needn't handle non-finite values. No bound on the sum of `leaf_pattern` on one device may be relied on, other than what follows from the above.
Results may differ from the reference program's by a relative error of at most 0.0001.
Values sent between devices are 32-bit elements; how exact they have to be, the bound alone decides.
A program may use at most 64 MiB of HBM per device.

```python
import math
import jax
import jax.numpy as jnp
from jax import lax

W0 = 1024
W1 = 512
W2 = 256
BLOCK = 128
POLES = 8
N1 = 8
NLEAF = 64
RB = 8
N_COL = 8


def draw_diagonal_block(key, lead_shape, order):
    first_key, second_key = jax.random.split(key, 2)
    normal_part = jnp.clip(jax.random.normal(first_key, lead_shape + (order, order), jnp.float32), -6.0, 6.0)
    offdiag = normal_part * (1.0 / math.sqrt(order))
    diagonal = jax.random.uniform(second_key, lead_shape + (order,), jnp.float32, 0.5, 2.0)
    return offdiag + diagonal[..., None] * jnp.eye(order, dtype=jnp.float32)


def draw_root_inverse(key, part):
    return draw_diagonal_block(jax.random.fold_in(key, 11), (POLES,), W0)


def draw_node_inverse(key, part):
    return draw_diagonal_block(jax.random.fold_in(key, 12), (POLES, N1), W1)


def draw_leaf_inverse(key, part):
    return draw_diagonal_block(jax.random.fold_in(key, 13), (POLES, NLEAF), W2)


def plant(result, stream_key, least, high):
    dims = result.shape
    place = [jax.random.randint(jax.random.fold_in(stream_key, axis), (), 0, dims[axis]) for axis in range(len(dims))]
    result = result.at[tuple(place)].set(least)
    longest = dims.index(max(dims))
    place[longest] = (place[longest] + 1) % dims[longest]
    return result.at[tuple(place)].set(high)


def levels(own_key, extent, cuts, smallest, top_value):
    factor_of = 1.0
    for position, parts in cuts:
        steps = jax.random.uniform(jax.random.fold_in(jax.random.fold_in(own_key, 6), position), (parts,), jnp.float32, smallest / len(cuts), top_value / len(cuts))
        factor_of = factor_of * jnp.repeat(jnp.exp(steps), extent[position] // parts).reshape((-1,) + (1,) * (len(extent) - 1 - position))
    return factor_of


def bell_draw(stream_key, shape, deviation, most, shards=(), held_as=jnp.bfloat16):
    factor_of = levels(stream_key, shape, shards, -0.22, 0.18) if shards else 1.0
    drawn = jax.random.normal(stream_key, shape, jnp.float32) * deviation * factor_of
    return jnp.minimum(jnp.maximum(drawn, -most), most).astype(held_as)


def setup_inputs(seed: int = 0) -> dict:
    splits = jax.random.split(jax.random.key(seed), 9)
    return {
        "root_inverse": draw_root_inverse(jax.random.fold_in(splits[8], 71), 0),
        "node_factor": bell_draw(splits[1], (POLES, N1, W0, W1), W0 ** -0.5, 0.1875, ((0, 4), (1, 8), (3, 8)), jnp.float32),
        "node_inverse": draw_node_inverse(jax.random.fold_in(splits[8], 71), 0),
        "leaf_root_factor": bell_draw(splits[3], (POLES, NLEAF, W0, W2), W0 ** -0.5, 0.1875, ((0, 4), (1, 64)), jnp.float32),
        "leaf_node_factor": bell_draw(splits[4], (POLES, NLEAF, W1, W2), W1 ** -0.5, 0.25, ((0, 4), (1, 64)), jnp.float32),
        "leaf_inverse": draw_leaf_inverse(jax.random.fold_in(splits[8], 71), 0),
        "leaf_pattern": plant((jax.random.randint(splits[6], (NLEAF, RB), 0, 2) < 1).astype(jnp.int32), jax.random.fold_in(splits[6], 1), 0, 1),
        "pole_weight": jnp.clip(jnp.exp(math.log(1.0) - 2.3025851 * jax.random.uniform(splits[7], (POLES,), jnp.float32) ** levels(splits[7], (POLES,), ((0, 4),), -0.2, 0.2)), 0.1, 1.0),
    }


highest = lax.Precision.HIGHEST


def product(left, right):
    return jnp.matmul(left, right, precision=highest)


def reference(root_inverse, node_factor, node_inverse, leaf_root_factor, leaf_node_factor, leaf_inverse, leaf_pattern, pole_weight):
    row_mask = jnp.repeat(leaf_pattern.astype(jnp.float32), BLOCK, axis=1)
    parent = jnp.arange(NLEAF, dtype=jnp.int32) // N_COL
    totals = None
    for pole_index in range(POLES):
        weight = pole_weight[pole_index]
        root_now = root_inverse[pole_index]
        factor_now = node_factor[pole_index]
        offdiag = -product(root_now[None], factor_now)
        sepdiag = node_inverse[pole_index] - product(jnp.swapaxes(factor_now, 1, 2), offdiag)
        masked = leaf_root_factor[pole_index] * row_mask[:, :, None]
        node_leaf = leaf_node_factor[pole_index]
        parent_off = offdiag[parent]
        parent_diag = sepdiag[parent]
        upper = -(product(root_now[None], masked) + product(parent_off, node_leaf))
        middle = -(product(jnp.swapaxes(parent_off, 1, 2), masked) + product(parent_diag, node_leaf))
        lower = leaf_inverse[pole_index] - product(jnp.swapaxes(masked, 1, 2), upper) - product(jnp.swapaxes(node_leaf, 1, 2), middle)
        terms = (root_now, offdiag, sepdiag, upper, middle, lower)
        terms = tuple(weight * item for item in terms)
        if totals is None:
            totals = terms
        else:
            totals = tuple(first + second for first, second in zip(totals, terms))
    return (totals[0], totals[1], totals[2], totals[3], totals[4], totals[5])
```

```python
import functools

import jax
import jax.numpy as jnp
from jax import lax
from jax.experimental import pallas as pl
from jax.experimental.pallas import tpu as pltpu
from jax.sharding import PartitionSpec as P

high = lax.Precision.HIGH
MESH = pl.DeviceIdType.MESH


def product(left, right):
    return jnp.matmul(left, right, precision=high)


def weighted(weights, values):
    return jnp.sum(weights[:, None, None] * values, axis=0)


def gather_kernel(
    n_row, n_x, r_ref, f_ref, rg, fg,
    near_send, near_recv, ring_send, ring_recv, pair_send, pair_recv,
    wide_send, wide_recv, mate_send, mate_recv, local_sem,
):
    pole, row, col = lax.axis_index("pole"), lax.axis_index("row"), lax.axis_index("col")
    x, core = col // 2, lax.rem(col, 2)
    other = 1 - core

    def at(dx, k):
        return (pole, row, lax.rem(x + dx + n_x, n_x) * 2 + k)

    up = (pole, lax.rem(row + 1, n_row), col)
    down = (pole, lax.rem(row + n_row - 1, n_row), col)
    mate = (pole, row, x * 2 + other)

    barrier = pltpu.get_barrier_semaphore()
    peers = [up, down, mate] + [at(dx, k) for dx in range(1, n_x) for k in range(2)]
    for peer in peers:
        pl.semaphore_signal(barrier, inc=1, device_id=peer, device_id_type=MESH)
    pl.semaphore_wait(barrier, len(peers))

    def remote(src, dst, ssem, rsem, dev):
        return pltpu.make_async_remote_copy(
            src_ref=src, dst_ref=dst, send_sem=ssem, recv_sem=rsem,
            device_id=dev, device_id_type=MESH,
        )

    own = pl.ds(pl.multiple_of(col * 16, 16), 16)
    keep = pltpu.make_async_copy(r_ref.at[core], rg.at[core, row, own], local_sem.at[0])
    keep.start()
    pending = []
    sent = []

    def near(dx, flip):
        k = other if flip else core
        return remote(
            r_ref.at[k], rg.at[k, row, own],
            near_send.at[dx, flip], near_recv.at[(n_x - dx) % n_x, flip], at(dx, k),
        )

    order = [0, 1, n_x - 1, 2]
    for dx in order:
        for flip in range(2):
            if dx == 0 and flip == 0:
                continue
            copy = near(dx, flip)
            copy.start()
            sent.append(copy)
    keep.wait()

    def chunk(block, i):
        start = pl.multiple_of(lax.rem(x + order[i], n_x) * 32, 32)
        return rg.at[core, block, pl.ds(start, 32)]

    def pass_to_mate(block, slot, i):
        copy = remote(
            chunk(block, i), chunk(block, i), pair_send.at[slot, i], pair_recv.at[slot, i], mate
        )
        copy.start()
        sent.append(copy)

    def mate_chunk_wait(slot, i):
        ref = rg.at[other, 0, pl.ds(0, 32)]
        remote(ref, ref, pair_send.at[slot, i], pair_recv.at[slot, i], mate).wait_recv()

    fown = pl.ds(pl.multiple_of(col * 64, 64), 64)
    last = 3
    for step in range(last + 2):
        for i in range(4):
            for way in range(2):
                if step == 0 and way == 1:
                    pass
                block = lax.rem(row + (n_row - step if way == 0 else step), n_row)
                if step == 0:
                    if way == 0:
                        dx = order[i]
                        for flip in range(2):
                            if dx == 0 and flip == 0:
                                continue
                            src = r_ref.at[0]
                            remote(
                                src, src, near_send.at[0, 0], near_recv.at[dx, flip], mate
                            ).wait_recv()
                else:
                    if step == last + 1 and (i < 2) != (way == 0):
                        continue
                    ref = chunk(block, i)
                    remote(
                        ref, ref, ring_send.at[way, step - 1, i], ring_recv.at[way, step - 1, i], mate
                    ).wait_recv()
                if step < last or (step == last and (i < 2) == (way == 0)):
                    copy = remote(
                        chunk(block, i), chunk(block, i),
                        ring_send.at[way, step, i], ring_recv.at[way, step, i],
                        up if way == 0 else down,
                    )
                    copy.start()
                    sent.append(copy)
                if step == 0:
                    if way == 0:
                        pass_to_mate(block, 0, i)
                elif step <= last:
                    pass_to_mate(block, 1 + 2 * (step - 1) + way, i)
                else:
                    pass_to_mate(block, 7, i)
        if step == 0:
            keep_f = pltpu.make_async_copy(f_ref, fg.at[:, fown], local_sem.at[1])
            keep_f.start()
            for dx in (1, n_x - 1, 2):
                copy = remote(
                    f_ref, fg.at[:, fown], wide_send.at[dx],
                    wide_recv.at[(n_x - dx) % n_x], at(dx, core),
                )
                copy.start()
                sent.append(copy)
            copy = remote(f_ref, fg.at[:, fown], mate_send.at[0], mate_recv.at[0], mate)
            copy.start()
            sent.append(copy)
            keep_f.wait()
    for dx in (1, n_x - 1, 2):
        there = pl.ds(pl.multiple_of(lax.rem(x + dx, n_x) * 128 + core * 64, 64), 64)
        ref = fg.at[:, there]
        remote(ref, ref, wide_send.at[dx], wide_recv.at[dx], mate).wait_recv()
        copy = remote(ref, ref, mate_send.at[dx], mate_recv.at[dx], mate)
        copy.start()
        sent.append(copy)
    for dx in range(n_x):
        remote(f_ref, f_ref, mate_send.at[dx], mate_recv.at[dx], mate).wait_recv()
    for slot in range(8):
        for i in range(4):
            mate_chunk_wait(slot, i)
    for copy in sent:
        copy.wait_send()


def gather(r, f, n_row, n_x):
    dma = pltpu.SemaphoreType.DMA
    return pl.pallas_call(
        functools.partial(gather_kernel, n_row, n_x),
        out_shape=(
            jax.ShapeDtypeStruct((2, n_row, 1024 // n_row, 1024), jnp.float32),
            jax.ShapeDtypeStruct((2, 512, 1024), jnp.float32),
        ),
        in_specs=[pl.BlockSpec(memory_space=pltpu.VMEM)] * 2,
        out_specs=[pl.BlockSpec(memory_space=pltpu.VMEM)] * 2,
        scratch_shapes=[
            dma((4, 2)), dma((4, 2)), dma((2, 4, 4)), dma((2, 4, 4)), dma((8, 4)), dma((8, 4)),
            dma((4,)), dma((4,)), dma((4,)), dma((4,)), dma((2,)),
        ],
        compiler_params=pltpu.CompilerParams(
            collective_id=0, has_side_effects=True, vmem_limit_bytes=32 << 20
        ),
    )(r, f)


PARTS = 5


def sum_kernel(a_ref, out, mid, fin, s0, r0, s1, r1, s2, r2, s3, r3):
    pole, row, col = lax.axis_index("pole"), lax.axis_index("row"), lax.axis_index("col")
    nxt, prv, opp = lax.rem(pole + 1, 4), lax.rem(pole + 3, 4), lax.rem(pole + 2, 4)
    to = ((nxt, row, col), (prv, row, col))
    owner = (nxt, prv)
    barrier = pltpu.get_barrier_semaphore()
    for peer in to:
        pl.semaphore_signal(barrier, inc=1, device_id=peer, device_id_type=MESH)
    pl.semaphore_wait(barrier, 2)

    def remote(src, dst, ssem, rsem, dev):
        return pltpu.make_async_remote_copy(
            src_ref=src, dst_ref=dst, send_sem=ssem, recv_sem=rsem,
            device_id=dev, device_id_type=MESH,
        )

    sent = []

    def go(copy):
        copy.start()
        sent.append(copy)

    for t in range(PARTS):
        for w in range(2):
            go(remote(a_ref.at[opp, w, t], mid.at[w, t], s0.at[w, t], r0.at[w, t], to[w]))
    for t in range(PARTS):
        for w in range(2):
            go(remote(a_ref.at[owner[w], 1 - w, t], fin.at[w, 1 - w, t],
                      s1.at[w, 1 - w, t], r1.at[w, 1 - w, t], to[w]))
        for w in range(2):
            ref = mid.at[w, t]
            remote(ref, ref, s0.at[w, t], r0.at[w, t], to[w]).wait_recv()
            mid[w, t] += a_ref[owner[w], w, t]
            go(remote(mid.at[w, t], fin.at[w, w, t], s1.at[w, w, t], r1.at[w, w, t], to[w]))
    for t in range(PARTS):
        for h in range(2):
            for w in range(2):
                ref = fin.at[w, h, t]
                remote(ref, ref, s1.at[w, h, t], r1.at[w, h, t], to[w]).wait_recv()
            out[pole, h, t] = a_ref[pole, h, t] + (fin[0, h, t] + fin[1, h, t])
        for w in range(2):
            for h in (w, 1 - w):
                go(remote(out.at[pole, h, t], out.at[pole, h, t],
                          s2.at[w, h, t], r2.at[w, h, t], to[w]))
    for t in range(PARTS):
        for w in range(2):
            src = prv if w == 0 else nxt
            ref = out.at[src, w, t]
            remote(ref, ref, s2.at[w, w, t], r2.at[w, w, t], to[w]).wait_recv()
            go(remote(ref, ref, s3.at[w, t], r3.at[w, t], to[w]))
    for t in range(PARTS):
        for w in range(2):
            ref = out.at[pole, 1 - w, t]
            remote(ref, ref, s2.at[w, 1 - w, t], r2.at[w, 1 - w, t], to[w]).wait_recv()
            remote(ref, ref, s3.at[w, t], r3.at[w, t], to[w]).wait_recv()
    for copy in sent:
        copy.wait_send()


def pole_sum(a):
    dma = pltpu.SemaphoreType.DMA
    n = a.shape[3]
    return pl.pallas_call(
        sum_kernel,
        out_shape=jax.ShapeDtypeStruct(a.shape, a.dtype),
        in_specs=[pl.BlockSpec(memory_space=pltpu.VMEM)],
        out_specs=pl.BlockSpec(memory_space=pltpu.VMEM),
        scratch_shapes=[
            pltpu.VMEM((2, PARTS, n, 256), jnp.float32),
            pltpu.VMEM((2, 2, PARTS, n, 256), jnp.float32),
            dma((2, PARTS)), dma((2, PARTS)), dma((2, 2, PARTS)), dma((2, 2, PARTS)),
            dma((2, 2, PARTS)), dma((2, 2, PARTS)), dma((2, PARTS)), dma((2, PARTS)),
        ],
        compiler_params=pltpu.CompilerParams(
            collective_id=1, has_side_effects=True, vmem_limit_bytes=32 << 20
        ),
    )(a)


def shards(
    n_row, n_x,
    root_inverse,
    node_factor,
    node_inverse,
    leaf_root_factor,
    leaf_node_factor,
    leaf_inverse,
    leaf_pattern,
    pole_weight,
):
    own_t = jnp.swapaxes(node_factor[:, 0], 1, 2)
    width = own_t.shape[1]
    node_inv = node_inverse[:, 0]
    node_leaf = leaf_node_factor[:, 0]
    leaf_inv = leaf_inverse[:, 0]
    block_rows = leaf_root_factor.shape[2] // leaf_pattern.shape[1]
    row_mask = jnp.repeat(leaf_pattern[0].astype(jnp.float32), block_rows)
    masked = leaf_root_factor[:, 0] * row_mask[None, :, None]
    root, factor_t = gather(root_inverse, own_t, n_row, n_x)
    root = root.reshape(2, 1024, 1024)
    col_index = lax.axis_index("col")
    own_rows = lax.dynamic_slice_in_dim(node_inv, col_index * width, width, 1)
    off = jnp.einsum("pij,pkj->pik", root, factor_t, precision=high)
    off_own = jnp.einsum("pkj,pij->pki", own_t, root, precision=high)
    times = product(root, masked)
    carried = product(off, node_leaf)
    upper = carried - times
    middle = (
        jnp.einsum("pij,pik->pjk", off, masked, precision=high)
        - product(node_inv, node_leaf)
        - product(factor_t, carried)
    )
    diag_rows = own_rows + product(own_t, off)
    lower = (
        leaf_inv
        - jnp.einsum("pij,pik->pjk", masked, upper, precision=high)
        - jnp.einsum("pij,pik->pjk", node_leaf, middle, precision=high)
    )
    terms = (
        weighted(pole_weight, root_inverse),
        weighted(pole_weight, -off_own),
        weighted(pole_weight, diag_rows),
        weighted(pole_weight, upper),
        weighted(pole_weight, middle),
        weighted(pole_weight, lower),
    )
    packed = jnp.concatenate([term.reshape(-1, 256) for term in terms], axis=0)
    total = pole_sum(packed.reshape(4, 2, PARTS, -1, 256)).reshape(-1, 256)
    outs, start = [], 0
    for term in terms:
        rows = term.size // 256
        outs.append(total[start:start + rows].reshape(term.shape))
        start += rows
    return (outs[0], outs[1].T[None], outs[2][None], outs[3][None], outs[4][None], outs[5][None])


def solution(mesh):
    return jax.shard_map(
        functools.partial(shards, mesh.shape["row"], mesh.shape["col"] // 2),
        mesh=mesh,
        in_specs=(
            P("pole", ("row", "col"), None),
            P("pole", "row", None, "col"),
            P("pole", "row", None, None),
            P("pole", ("row", "col"), None, None),
            P("pole", ("row", "col"), None, None),
            P("pole", ("row", "col"), None, None),
            P(("row", "col"), None),
            P("pole"),
        ),
        out_specs=(
            P(("row", "col"), None),
            P("row", None, "col"),
            P("row", "col", None),
            P(("row", "col"), None, None),
            P(("row", "col"), None, None),
            P(("row", "col"), None, None),
        ),
        check_vma=False,
    )
```

```python
import functools

import jax
import jax.numpy as jnp
from jax import lax
from jax.experimental import pallas as pl
from jax.experimental.pallas import tpu as pltpu
from jax.sharding import PartitionSpec as P

MESH = pl.DeviceIdType.MESH
F32, BF16 = jnp.float32, jnp.bfloat16
ROWS, WIDE, LEAF = 1024, 512, 256
Z, X = 8, 4


def split(value):
    hi = value.astype(BF16)
    return hi, (value - hi.astype(F32)).astype(BF16)


def nn(left, right):
    return lax.dot_general(left, right, (((1,), (0,)), ((), ())), preferred_element_type=F32)


def nt(left, right):
    return lax.dot_general(left, right, (((1,), (1,)), ((), ())), preferred_element_type=F32)


def three(dot, stacked, hi, lo):
    half = stacked.shape[0] // 2
    both = dot(stacked, hi)
    return both[:half] + both[half:] + dot(stacked[:half], lo)


class Part:
    def __init__(self, index, shape, mid, fin, src, out):
        self.index, self.shape, self.mid, self.fin, self.src, self.out = index, shape, mid, fin, src, out


def kernel(
    pat, weight, r_ref, f_ref, d_hbm, a_hbm, n_hbm, l_hbm, dw_hbm,
    rb, no, nd, lr, ln, ld,
    dbuf, abuf, nbuf, lbuf, dwbuf,
    rg, fg, ft, fohl, whi, wlo, nhi, nlo, nthl, dn, mt, rhl, ghl,
    ups, offd, offo, diag, rootw, lnw, low,
    mids, fins, omid, ofin, gmid, gfin, rmid, rfin,
    near_send, near_recv, ring_send, ring_recv, pair_send, pair_recv,
    fw_send, fw_recv, fx_send, fx_recv, mate_send, mate_recv, local_sem,
    s0, q0, s1, q1, s2, q2, s3, q3,
):
    pole, row, col = lax.axis_index("pole"), lax.axis_index("row"), lax.axis_index("col")
    x, core = col // 2, lax.rem(col, 2)
    other = 1 - core

    loads = []
    for k, (src, dst) in enumerate(
        ((a_hbm, abuf), (n_hbm, nbuf), (d_hbm, dbuf), (l_hbm, lbuf), (dw_hbm, dwbuf))
    ):
        copy = pltpu.make_async_copy(src, dst, local_sem.at[k])
        copy.start()
        loads.append(copy)

    def at(dx, k):
        return (pole, row, lax.rem(x + dx + X, X) * 2 + k)

    along = ((pole, lax.rem(row + 1, Z), col), (pole, lax.rem(row + Z - 1, Z), col))
    beside = (at(1, core), at(X - 1, core))
    mate = (pole, row, x * 2 + other)
    nxt, prv, opp = lax.rem(pole + 1, 4), lax.rem(pole + 3, 4), lax.rem(pole + 2, 4)
    turn = ((nxt, row, col), (prv, row, col))
    owner = (nxt, prv)

    barrier = pltpu.get_barrier_semaphore()
    peers = [*along, mate, *turn] + [at(dx, k) for dx in range(1, X) for k in range(2)]
    for peer in peers:
        pl.semaphore_signal(barrier, inc=1, device_id=peer, device_id_type=MESH)
    pl.semaphore_wait(barrier, len(peers))

    def remote(src, dst, ssem, rsem, dev):
        return pltpu.make_async_remote_copy(
            src_ref=src, dst_ref=dst, send_sem=ssem, recv_sem=rsem,
            device_id=dev, device_id_type=MESH,
        )

    sent = []

    def go(src, dst, ssem, rsem, dev):
        copy = remote(src, dst, ssem, rsem, dev)
        copy.start()
        sent.append(copy)

    def got(ref, ssem, rsem):
        remote(ref, ref, ssem, rsem, mate).wait_recv()

    own = pl.ds(pl.multiple_of(col * 16, 16), 16)
    for dx in range(X):
        for flip in range(2):
            if dx or flip:
                k = other if flip else core
                go(r_ref.at[k], rg.at[k, row, own], near_send.at[dx, flip],
                   near_recv.at[(X - dx) % X, flip], at(dx, k))
    rg[core, row, own] = r_ref[core]

    def chunk(block, i):
        start = pl.multiple_of(lax.rem(x + i, X) * 32, 32)
        return rg.at[core, block, pl.ds(start, 32)]

    def to_mate(block, slot, i):
        go(chunk(block, i), chunk(block, i), pair_send.at[slot, i], pair_recv.at[slot, i], mate)

    def forward(step, i, way, block):
        if step < 3 or (step == 3 and (i < 2) == (way == 0)):
            go(chunk(block, i), chunk(block, i), ring_send.at[way, step, i],
               ring_recv.at[way, step, i], along[way])

    def block_of(step, way):
        return lax.rem(row + (Z - step if way == 0 else step), Z)

    def event(step, i):
        if step == 0:
            for flip in range(2):
                if i or flip:
                    got(r_ref.at[0], near_send.at[0, 0], near_recv.at[i, flip])
            for way in range(2):
                forward(0, i, way, row)
            to_mate(row, 0, i)
            return
        for way in range(2):
            if step == 4 and (i < 2) != (way == 0):
                continue
            block = block_of(step, way)
            got(chunk(block, i), ring_send.at[way, step - 1, i], ring_recv.at[way, step - 1, i])
            forward(step, i, way, block)
            to_mate(block, 7 if step == 4 else 1 + 2 * (step - 1) + way, i)

    def mate_wait(slot):
        for i in range(4):
            got(rg.at[other, 0, pl.ds(0, 32)], pair_send.at[slot, i], pair_recv.at[slot, i])

    def frows(dx, start=0, size=64):
        first = lax.rem(x + dx, X) * 128 + core * 64 + start
        return pl.ds(pl.multiple_of(first, 32), size)

    def f_start(p):
        here = fg.at[p, frows(0)]
        for way in range(2):
            go(ft.at[p], here, fw_send.at[p, way], fw_recv.at[p, way], beside[way])
        go(ft.at[p], here, mate_send.at[p, 0], mate_recv.at[p, 0], mate)

    def f_relay(p):
        for way, dx in ((0, X - 1), (1, 1)):
            ref = fg.at[p, frows(dx)]
            got(ref, fw_send.at[p, way], fw_recv.at[p, way])
            part = fg.at[p, frows(dx, 32 * way, 32)]
            go(part, part, fx_send.at[p, way], fx_recv.at[p, way], beside[way])
            go(ref, ref, mate_send.at[p, 1 + way], mate_recv.at[p, 1 + way], mate)

    def f_last(p):
        for way in range(2):
            got(fg.at[p, frows(2, 32 * way, 32)], fx_send.at[p, way], fx_recv.at[p, way])
        ref = fg.at[p, frows(2)]
        go(ref, ref, mate_send.at[p, 3], mate_recv.at[p, 3], mate)

    def f_use(p):
        for k in range(4):
            got(ft.at[p], mate_send.at[p, k], mate_recv.at[p, k])

        def body(i, _):
            rows = pl.ds(pl.multiple_of(i * 64, 64), 64)
            whi[p, rows], wlo[p, rows] = split(fg[p, rows])
            return 0

        lax.fori_loop(0, 8, body, 0)

    def prep_f(p):
        t = jnp.transpose(f_ref[p])
        ft[p] = t
        fg[p, frows(0)] = t
        fohl[p, 0:64], fohl[p, 64:128] = split(t)

    def prep_a(p):
        for i in range(8):
            t = jnp.transpose(abuf[p, 128 * i:128 * i + 128] * pat[0, i].astype(F32))
            cols = slice(128 * i, 128 * i + 128)
            whi[p, WIDE:, cols], wlo[p, WIDE:, cols] = split(t)

    def prep_n(p):
        n = nbuf[p]
        nhi[p], nlo[p] = split(n)
        nthl[p, 0:LEAF], nthl[p, LEAF:] = split(jnp.transpose(n))

    def prep_d(p):
        for i in range(2):
            rows = slice(256 * i, 256 * i + 256)
            hi, lo = split(dbuf[p, rows])
            dn[p, rows] = nn(hi, nhi[p]) + nn(lo, nhi[p]) + nn(hi, nlo[p])

    def blocks(t):
        return lax.rem(row + t, Z), lax.rem(row + Z - t - 1, Z)

    def pair_cols(get, t):
        b1, b2 = blocks(t)
        return jnp.concatenate(
            [get(pl.ds(pl.multiple_of(b * 128, 128), 128)) for b in (b1, b2)], axis=1
        )

    def piece(t, p):
        w = weight[p]
        for k, b in enumerate(blocks(t)):
            hi, lo = split(rg[p, b])
            rhl[128 * k:128 * k + 128] = hi
            rhl[256 + 128 * k:384 + 128 * k] = lo
        for n in range(2):
            rows = slice(256 * n, 256 * n + 256)
            g = three(nt, rhl[...], whi[p, rows], wlo[p, rows])
            ghl[0:256, rows], ghl[256:512, rows] = split(g)
        times = three(nt, rhl[...], whi[p, WIDE:], wlo[p, WIDE:])
        o = three(nt, fohl[p], rhl[0:256], rhl[256:512])
        y = three(nn, ghl[...], nhi[p], nlo[p])
        up = y - times
        if p == 0:
            ups[t] = w * up
            offd[t] = -(w * o)
        else:
            ups[t] += w * up
            offd[t] -= w * o
        ath = pair_cols(lambda c: whi[p, WIDE:, c], t)
        atl = pair_cols(lambda c: wlo[p, WIDE:, c], t)
        at2 = jnp.concatenate([ath, atl], axis=0)
        yth, ytl = split(jnp.transpose(y))
        yt2 = jnp.concatenate([yth, ytl], axis=0)
        fth = pair_cols(lambda c: whi[p, :WIDE, c], t)
        ftl = pair_cols(lambda c: wlo[p, :WIDE, c], t)
        m = three(nn, at2, ghl[0:256], ghl[256:512]) - three(nt, yt2, fth, ftl)
        uh, ul = split(up)
        e = w * three(nn, at2, uh, ul)
        fo2 = pair_cols(lambda c: fohl[p, :, c], t)
        g2 = w * three(nn, fo2, ghl[0:256], ghl[256:512])
        if t == 0:
            mt[p] = m
        else:
            mt[p] += m
        low[...] -= e
        diag[...] += g2

    parts = {}

    def add_part(name, index, mid, fin, src, out):
        parts[name] = Part(index, None, mid, fin, src, out)

    def stage0(name):
        part = parts[name]
        n = part.index
        for w in range(2):
            go(part.src(opp, w), part.mid(w), s0.at[n, w], q0.at[n, w], turn[w])
        for w in range(2):
            go(part.src(owner[w], 1 - w), part.fin(w, 1 - w),
               s1.at[n, w, 1 - w], q1.at[n, w, 1 - w], turn[w])

    def stage1(name):
        part = parts[name]
        n = part.index
        for w in range(2):
            ref = part.mid(w)
            got(ref, s0.at[n, w], q0.at[n, w])
            ref[...] += part.src(owner[w], w)[...]
            go(ref, part.fin(w, w), s1.at[n, w, w], q1.at[n, w, w], turn[w])

    def stage2(name):
        part = parts[name]
        n = part.index
        for h in range(2):
            for w in range(2):
                got(part.fin(w, h), s1.at[n, w, h], q1.at[n, w, h])
            ref = part.out(pole, h)
            ref[...] = part.src(pole, h)[...] + (part.fin(0, h)[...] + part.fin(1, h)[...])
        for w in range(2):
            for h in (w, 1 - w):
                ref = part.out(pole, h)
                go(ref, ref, s2.at[n, w, h], q2.at[n, w, h], turn[w])

    def stage3(name):
        part = parts[name]
        n = part.index
        for w in range(2):
            ref = part.out(prv if w == 0 else nxt, w)
            got(ref, s2.at[n, w, w], q2.at[n, w, w])
            go(ref, ref, s3.at[n, w], q3.at[n, w], turn[w])

    def stage4(name):
        part = parts[name]
        n = part.index
        for w in range(2):
            ref = part.out(pole, 1 - w)
            got(ref, s2.at[n, w, 1 - w], q2.at[n, w, 1 - w])
            got(ref, s3.at[n, w], q3.at[n, w])

    def m32(v):
        return pl.ds(pl.multiple_of(v, 32), 32)

    def m8(v):
        return pl.ds(pl.multiple_of(v, 8), 8)

    for t in range(4):
        b1, b2 = blocks(t)

        def lr_out(q, h, b1=b1, b2=b2):
            side = q // 2
            return lr.at[m32((b1 + side * (b2 - b1)) * 128 + lax.rem(q, 2) * 64 + h * 32)]

        add_part("lr%d" % t, t, lambda w, t=t: mids.at[t, w], lambda w, h, t=t: fins.at[t, w, h],
                 lambda q, h, t=t: ups.at[t, m32(q * 64 + h * 32)], lr_out)
    for j in range(2):
        n = 4 + j
        add_part("ln%d" % j, n, lambda w, n=n: mids.at[n, w], lambda w, h, n=n: fins.at[n, w, h],
                 lambda q, h, j=j: lnw.at[m32(j * 256 + q * 64 + h * 32)],
                 lambda q, h, j=j: ln.at[m32(j * 256 + q * 64 + h * 32)])
    add_part("ld", 6, lambda w: mids.at[6, w], lambda w, h: fins.at[6, w, h],
             lambda q, h: low.at[m32(q * 64 + h * 32)], lambda q, h: ld.at[m32(q * 64 + h * 32)])
    for n, ts in ((7, pl.ds(0, 3)), (8, pl.ds(3, 1))):
        add_part("of%d" % n, n, lambda w, ts=ts: omid.at[w, ts], lambda w, h, ts=ts: ofin.at[w, h, ts],
                 lambda q, h, ts=ts: offd.at[ts, m8(q * 16 + h * 8)],
                 lambda q, h, ts=ts: offo.at[ts, m8(q * 16 + h * 8)])
    add_part("nd", 9, lambda w: gmid.at[w], lambda w, h: gfin.at[w, h],
             lambda q, h: diag.at[m8(q * 16 + h * 8)], lambda q, h: nd.at[m8(q * 16 + h * 8)])

    def lanes(q, h):
        return pl.ds(pl.multiple_of(q * 256 + h * 128, 128), 128)

    add_part("rb", 10, lambda w: rmid.at[w], lambda w, h: rfin.at[w, h],
             lambda q, h: rootw.at[:, lanes(q, h)], lambda q, h: rb.at[:, lanes(q, h)])

    def finish(p):
        w = weight[p]
        mid = jnp.transpose(mt[p]) - dn[p]
        if p == 0:
            lnw[...] = w * mid
        else:
            lnw[...] += w * mid
        ghl[:, 0:256], ghl[:, 256:512] = split(mid)

    def finish_low(p):
        low[...] -= weight[p] * three(nn, nthl[p], ghl[:, 0:256], ghl[:, 256:512])

    def offdiag_out(ts):
        for t in ts:
            for k, b in enumerate(blocks(t)):
                no[pl.ds(pl.multiple_of(b * 128, 128), 128)] = jnp.transpose(
                    offo[t, :, 128 * k:128 * k + 128]
                )

    event(0, 0)
    prep_f(0)
    event(0, 1)
    prep_f(1)
    event(0, 2)
    event(0, 3)
    f_start(0)
    rootw[...] = weight[0] * r_ref[0] + weight[1] * r_ref[1]
    stage0("rb")
    loads[0].wait()
    prep_a(0)
    event(1, 0)
    f_start(1)
    prep_a(1)
    event(1, 1)
    f_relay(0)
    loads[1].wait()
    prep_n(0)
    stage1("rb")
    event(1, 2)
    prep_n(1)
    loads[2].wait()
    prep_d(0)
    event(1, 3)
    stage2("rb")
    f_last(0)
    prep_d(1)
    event(2, 0)
    f_relay(1)
    loads[3].wait()
    loads[4].wait()
    low[...] = weight[0] * lbuf[0] + weight[1] * lbuf[1]
    diag[...] = weight[0] * dwbuf[0] + weight[1] * dwbuf[1]
    f_use(0)
    mate_wait(0)
    mate_wait(1)
    piece(0, 0)
    stage3("rb")
    event(2, 1)
    f_last(1)
    event(2, 2)
    f_use(1)
    piece(0, 1)
    stage0("lr0")
    event(2, 3)
    event(3, 0)
    mate_wait(2)
    mate_wait(3)
    piece(1, 0)
    stage1("lr0")
    event(3, 1)
    piece(1, 1)
    stage0("lr1")
    stage2("lr0")
    event(3, 2)
    event(3, 3)
    mate_wait(4)
    mate_wait(5)
    piece(2, 0)
    stage1("lr1")
    stage3("lr0")
    event(4, 0)
    event(4, 2)
    piece(2, 1)
    stage0("lr2")
    stage0("of7")
    stage2("lr1")
    event(4, 1)
    event(4, 3)
    mate_wait(6)
    mate_wait(7)
    piece(3, 0)
    stage1("lr2")
    stage1("of7")
    stage3("lr1")
    piece(3, 1)
    for name in ("lr3", "of8", "nd"):
        stage0(name)
    stage2("lr2")
    stage2("of7")
    finish(0)
    finish_low(0)
    finish(1)
    stage0("ln0")
    stage0("ln1")
    for name in ("lr3", "of8", "nd"):
        stage1(name)
    finish_low(1)
    stage0("ld")
    stage3("lr2")
    stage3("of7")
    for name in ("lr3", "of8", "nd"):
        stage2(name)
    for name in ("ln0", "ln1", "ld"):
        stage1(name)
    for name in ("lr3", "of8", "nd"):
        stage3(name)
    for name in ("ln0", "ln1", "ld"):
        stage2(name)
    stage4("of7")
    offdiag_out(range(3))
    for name in ("ln0", "ln1", "ld"):
        stage3(name)
    stage4("of8")
    offdiag_out(range(3, 4))
    for name in ("rb", "lr0", "lr1", "lr2", "lr3", "nd", "ln0", "ln1", "ld"):
        stage4(name)
    for copy in sent:
        copy.wait_send()


def sweep(pattern, weights, root, factor, node_inv, leaf_root, node_leaf, leaf_inv, own_rows):
    dma = pltpu.SemaphoreType.DMA
    vmem = pltpu.VMEM
    f32 = lambda *shape: vmem(shape, F32)
    bf16 = lambda *shape: vmem(shape, BF16)
    n = 11
    return pl.pallas_call(
        kernel,
        out_shape=tuple(
            jax.ShapeDtypeStruct(shape, F32)
            for shape in ((16, ROWS), (ROWS, 64), (64, WIDE), (ROWS, LEAF), (WIDE, LEAF), (LEAF, LEAF))
        ),
        in_specs=[pl.BlockSpec(memory_space=pltpu.SMEM)] * 2
        + [pl.BlockSpec(memory_space=pltpu.VMEM)] * 2
        + [pl.BlockSpec(memory_space=pl.ANY)] * 5,
        out_specs=[pl.BlockSpec(memory_space=pltpu.VMEM)] * 6,
        scratch_shapes=[
            f32(2, WIDE, WIDE), f32(2, ROWS, LEAF), f32(2, WIDE, LEAF), f32(2, LEAF, LEAF), f32(2, 64, WIDE),
            f32(2, Z, 128, ROWS), f32(2, WIDE, ROWS), f32(2, 64, ROWS), bf16(2, 128, ROWS),
            bf16(2, WIDE + LEAF, ROWS), bf16(2, WIDE + LEAF, ROWS),
            bf16(2, WIDE, LEAF), bf16(2, WIDE, LEAF), bf16(2, 2 * LEAF, WIDE),
            f32(2, WIDE, LEAF), f32(2, LEAF, WIDE), bf16(512, ROWS), bf16(512, WIDE),
            f32(4, 256, LEAF), f32(4, 64, 256), f32(4, 64, 256), f32(64, WIDE), f32(16, ROWS),
            f32(WIDE, LEAF), f32(LEAF, LEAF),
            f32(7, 2, 32, LEAF), f32(7, 2, 2, 32, LEAF), f32(2, 4, 8, 256), f32(2, 2, 4, 8, 256),
            f32(2, 8, WIDE), f32(2, 2, 8, WIDE), f32(2, 16, 128), f32(2, 2, 16, 128),
            dma((4, 2)), dma((4, 2)), dma((2, 4, 4)), dma((2, 4, 4)), dma((8, 4)), dma((8, 4)),
            dma((2, 2)), dma((2, 2)), dma((2, 2)), dma((2, 2)), dma((2, 4)), dma((2, 4)), dma((5,)),
            dma((n, 2)), dma((n, 2)), dma((n, 2, 2)), dma((n, 2, 2)),
            dma((n, 2, 2)), dma((n, 2, 2)), dma((n, 2)), dma((n, 2)),
        ],
        compiler_params=pltpu.CompilerParams(
            collective_id=0, has_side_effects=True, vmem_limit_bytes=58 << 20
        ),
    )(pattern, weights, root, factor, node_inv, leaf_root, node_leaf, leaf_inv, own_rows)


def shards(
    root_inverse,
    node_factor,
    node_inverse,
    leaf_root_factor,
    leaf_node_factor,
    leaf_inverse,
    leaf_pattern,
    pole_weight,
):
    node_inv = node_inverse[:, 0]
    own_rows = lax.dynamic_slice_in_dim(node_inv, lax.axis_index("col") * 64, 64, 1)
    outs = sweep(
        leaf_pattern, pole_weight, root_inverse, node_factor[:, 0], node_inv,
        leaf_root_factor[:, 0], leaf_node_factor[:, 0], leaf_inverse[:, 0], own_rows,
    )
    return (outs[0],) + tuple(out[None] for out in outs[1:])


def solution(mesh):
    return jax.shard_map(
        shards,
        mesh=mesh,
        in_specs=(
            P("pole", ("row", "col"), None),
            P("pole", "row", None, "col"),
            P("pole", "row", None, None),
            P("pole", ("row", "col"), None, None),
            P("pole", ("row", "col"), None, None),
            P("pole", ("row", "col"), None, None),
            P(("row", "col"), None),
            P("pole"),
        ),
        out_specs=(
            P(("row", "col"), None),
            P("row", None, "col"),
            P("row", "col", None),
            P(("row", "col"), None, None),
            P(("row", "col"), None, None),
            P(("row", "col"), None, None),
        ),
        check_vma=False,
    )
```

```python
import functools

import jax
import jax.numpy as jnp
from jax import lax
from jax.experimental import pallas as pl
from jax.experimental.pallas import tpu as pltpu
from jax.sharding import PartitionSpec as P

MESH = pl.DeviceIdType.MESH
F32, BF16 = jnp.float32, jnp.bfloat16
ROWS, WIDE, LEAF = 1024, 512, 256
Z, X = 8, 4


def split(value):
    hi = value.astype(BF16)
    return hi, (value - hi.astype(F32)).astype(BF16)


def nn(left, right):
    return lax.dot_general(left, right, (((1,), (0,)), ((), ())), preferred_element_type=F32)


def nt(left, right):
    return lax.dot_general(left, right, (((1,), (1,)), ((), ())), preferred_element_type=F32)


def three(dot, stacked, hi, lo):
    half = stacked.shape[0] // 2
    both = dot(stacked, hi)
    return both[:half] + both[half:] + dot(stacked[:half], lo)


class Part:
    def __init__(self, index, shape, mid, fin, src, out):
        self.index, self.shape, self.mid, self.fin, self.src, self.out = index, shape, mid, fin, src, out


def kernel(
    pat, weight, r_ref, ft, d_hbm, a_hbm, n_hbm, l_hbm,
    rb, no, nd, lr, ln, ld,
    dbuf, abuf, nbuf, lbuf,
    rg, fg, fohl, whi, wlo, nhi, nlo, nthl, dn, mt, rhl, ghl,
    ups, offd, offo, diag, rootw, lnw, low,
    mids, fins, omid, ofin, gmid, gfin, rmid, rfin,
    near_send, near_recv, ring_send, ring_recv, pair_send, pair_recv,
    cross_send, cross_recv, fw_send, fw_recv, fx_send, fx_recv, mate_send, mate_recv, local_sem,
    s0, q0, s1, q1, s2, q2, s3, q3,
):
    pole, row, col = lax.axis_index("pole"), lax.axis_index("row"), lax.axis_index("col")
    x, core = col // 2, lax.rem(col, 2)
    other = 1 - core

    loads = []
    for k, (src, dst) in enumerate(
        ((a_hbm, abuf), (n_hbm, nbuf), (d_hbm, dbuf), (l_hbm, lbuf))
    ):
        copy = pltpu.make_async_copy(src, dst, local_sem.at[k])
        copy.start()
        loads.append(copy)

    def at(dx, k):
        return (pole, row, lax.rem(x + dx + X, X) * 2 + k)

    along = ((pole, lax.rem(row + 1, Z), col), (pole, lax.rem(row + Z - 1, Z), col))
    beside = (at(1, core), at(X - 1, core))
    mate = (pole, row, x * 2 + other)
    nxt, prv, opp = lax.rem(pole + 1, 4), lax.rem(pole + 3, 4), lax.rem(pole + 2, 4)
    turn = ((nxt, row, col), (prv, row, col))
    owner = (nxt, prv)

    barrier = pltpu.get_barrier_semaphore()
    peers = [*along, mate, *turn] + [at(dx, k) for dx in range(1, X) for k in range(2)]
    for peer in peers:
        pl.semaphore_signal(barrier, inc=1, device_id=peer, device_id_type=MESH)
    pl.semaphore_wait(barrier, len(peers))

    def remote(src, dst, ssem, rsem, dev):
        return pltpu.make_async_remote_copy(
            src_ref=src, dst_ref=dst, send_sem=ssem, recv_sem=rsem,
            device_id=dev, device_id_type=MESH,
        )

    sent = []

    def go(src, dst, ssem, rsem, dev):
        copy = remote(src, dst, ssem, rsem, dev)
        copy.start()
        sent.append(copy)

    def got(ref, ssem, rsem):
        remote(ref, ref, ssem, rsem, mate).wait_recv()

    own = pl.ds(pl.multiple_of(col * 16, 16), 16)
    for dx in range(X):
        for flip in range(2):
            if dx or flip:
                k = other if flip else core
                go(r_ref.at[k], rg.at[k, row, own], near_send.at[dx, flip],
                   near_recv.at[(X - dx) % X, flip], at(dx, k))
    rg[core, row, own] = r_ref[core]

    def chunk(block, i):
        start = pl.multiple_of(lax.rem(x + i, X) * 32, 32)
        return rg.at[core, block, pl.ds(start, 32)]

    def to_mate(block, slot, i):
        go(chunk(block, i), chunk(block, i), pair_send.at[slot, i], pair_recv.at[slot, i], mate)

    def forward(step, i, way, block):
        if step < 2 or (step == 2 and i < 2) or (step == 3 and i == way):
            go(chunk(block, i), chunk(block, i), ring_send.at[way, step, i],
               ring_recv.at[way, step, i], along[way])

    def block_of(step, way):
        return lax.rem(row + (Z - step if way == 0 else step), Z)

    def event(step, i):
        if step == 0:
            for flip in range(2):
                if i or flip:
                    got(r_ref.at[0], near_send.at[0, 0], near_recv.at[i, flip])
            for way in range(2):
                forward(0, i, way, row)
            to_mate(row, 0, i)
            return
        for way in range(2):
            if step == 4 and i != way:
                continue
            block = block_of(step, way)
            slot = 7 if step == 4 else 1 + 2 * (step - 1) + way
            got(chunk(block, i), ring_send.at[way, step - 1, i], ring_recv.at[way, step - 1, i])
            forward(step, i, way, block)
            if step > 2:
                go(chunk(block, i), chunk(block, i), cross_send.at[slot - 5, i],
                   cross_recv.at[slot - 5, i], beside[i])
            to_mate(block, slot, i)

    def cross(slot):
        block = block_of(4 if slot == 7 else 3, (slot - 5) % 2)
        for i in range(2):
            ref = chunk(block, 3 - i)
            got(ref, cross_send.at[slot - 5, i], cross_recv.at[slot - 5, i])
            to_mate(block, slot, 3 - i)

    def mate_wait(slot):
        for i in range(4):
            got(rg.at[other, 0, pl.ds(0, 32)], pair_send.at[slot, i], pair_recv.at[slot, i])

    def frows(dx, start=0, size=64):
        first = lax.rem(x + dx, X) * 128 + core * 64 + start
        return pl.ds(pl.multiple_of(first, 32), size)

    def f_start(p):
        here = fg.at[p, frows(0)]
        for way in range(2):
            go(ft.at[p], here, fw_send.at[p, way], fw_recv.at[p, way], beside[way])
        go(ft.at[p], here, mate_send.at[p, 0], mate_recv.at[p, 0], mate)

    def f_relay(p):
        for way, dx in ((0, X - 1), (1, 1)):
            ref = fg.at[p, frows(dx)]
            got(ref, fw_send.at[p, way], fw_recv.at[p, way])
            part = fg.at[p, frows(dx, 32 * way, 32)]
            go(part, part, fx_send.at[p, way], fx_recv.at[p, way], beside[way])
            go(ref, ref, mate_send.at[p, 1 + way], mate_recv.at[p, 1 + way], mate)

    def f_last(p):
        for way in range(2):
            got(fg.at[p, frows(2, 32 * way, 32)], fx_send.at[p, way], fx_recv.at[p, way])
        ref = fg.at[p, frows(2)]
        go(ref, ref, mate_send.at[p, 3], mate_recv.at[p, 3], mate)

    def f_use(p):
        for k in range(4):
            got(ft.at[p], mate_send.at[p, k], mate_recv.at[p, k])

        def body(i, _):
            rows = pl.ds(pl.multiple_of(i * 64, 64), 64)
            whi[p, rows], wlo[p, rows] = split(fg[p, rows])
            return 0

        lax.fori_loop(0, 8, body, 0)

    def prep_f(p):
        t = ft[p]
        fg[p, frows(0)] = t
        fohl[p, 0:64], fohl[p, 64:128] = split(t)

    def prep_a(p):
        for i in range(8):
            t = jnp.transpose(abuf[p, 128 * i:128 * i + 128] * pat[0, i].astype(F32))
            cols = slice(128 * i, 128 * i + 128)
            whi[p, WIDE:, cols], wlo[p, WIDE:, cols] = split(t)

    def prep_n(p):
        n = nbuf[p]
        nhi[p], nlo[p] = split(n)
        nthl[p, 0:LEAF], nthl[p, LEAF:] = split(jnp.transpose(n))

    def prep_d(p):
        for i in range(2):
            rows = slice(256 * i, 256 * i + 256)
            hi, lo = split(dbuf[p, rows])
            dn[p, rows] = nn(hi, nhi[p]) + nn(lo, nhi[p]) + nn(hi, nlo[p])

    def blocks(t):
        first = lax.rem(row + t, Z)
        return [first] if t > 2 else [first, lax.rem(row + Z - t - 1, Z)]

    FIRST = (0, 256, 512, 768, 896)

    def pair_cols(get, t):
        cols = [get(pl.ds(pl.multiple_of(b * 128, 128), 128)) for b in blocks(t)]
        return cols[0] if len(cols) == 1 else jnp.concatenate(cols, axis=1)

    def piece(t, p):
        w = weight[p]
        size = 128 * len(blocks(t))
        here = slice(FIRST[t], FIRST[t] + size)
        top, all_rows = slice(0, size), slice(0, 2 * size)
        for k, b in enumerate(blocks(t)):
            hi, lo = split(rg[p, b])
            rhl[128 * k:128 * k + 128] = hi
            rhl[size + 128 * k:size + 128 * k + 128] = lo
        for n in range(2):
            rows = slice(256 * n, 256 * n + 256)
            g = three(nt, rhl[all_rows], whi[p, rows], wlo[p, rows])
            ghl[top, rows], ghl[size:2 * size, rows] = split(g)
        times = three(nt, rhl[all_rows], whi[p, WIDE:], wlo[p, WIDE:])
        y = three(nn, ghl[all_rows], nhi[p], nlo[p])
        up = y - times
        o = three(nt, fohl[p], rhl[top], rhl[size:2 * size])
        if p == 0:
            ups[here] = w * up
            offd[:, here] = -(w * o)
        else:
            ups[here] += w * up
            offd[:, here] -= w * o
        ath = pair_cols(lambda c: whi[p, WIDE:, c], t)
        atl = pair_cols(lambda c: wlo[p, WIDE:, c], t)
        at2 = jnp.concatenate([ath, atl], axis=0)
        yth, ytl = split(jnp.transpose(y))
        yt2 = jnp.concatenate([yth, ytl], axis=0)
        fth = pair_cols(lambda c: whi[p, :WIDE, c], t)
        ftl = pair_cols(lambda c: wlo[p, :WIDE, c], t)
        m = three(nn, at2, ghl[top], ghl[size:2 * size]) - three(nt, yt2, fth, ftl)
        uh, ul = split(up)
        e = w * three(nn, at2, uh, ul)
        fo2 = pair_cols(lambda c: fohl[p, :, c], t)
        g2 = w * three(nn, fo2, ghl[top], ghl[size:2 * size])
        if t == 0:
            mt[p] = m
        else:
            mt[p] += m
        low[...] -= e
        diag[...] += g2

    parts = {}

    def add_part(name, index, mid, fin, src, out):
        parts[name] = Part(index, None, mid, fin, src, out)

    def stage0(name):
        part = parts[name]
        n = part.index
        for w in range(2):
            go(part.src(opp, w), part.mid(w), s0.at[n, w], q0.at[n, w], turn[w])
        for w in range(2):
            go(part.src(owner[w], 1 - w), part.fin(w, 1 - w),
               s1.at[n, w, 1 - w], q1.at[n, w, 1 - w], turn[w])

    def stage1(name):
        part = parts[name]
        n = part.index
        for w in range(2):
            ref = part.mid(w)
            got(ref, s0.at[n, w], q0.at[n, w])
            ref[...] += part.src(owner[w], w)[...]
            go(ref, part.fin(w, w), s1.at[n, w, w], q1.at[n, w, w], turn[w])

    def stage2(name):
        part = parts[name]
        n = part.index
        for h in range(2):
            for w in range(2):
                got(part.fin(w, h), s1.at[n, w, h], q1.at[n, w, h])
            ref = part.out(pole, h)
            ref[...] = part.src(pole, h)[...] + (part.fin(0, h)[...] + part.fin(1, h)[...])
        for w in range(2):
            for h in (w, 1 - w):
                ref = part.out(pole, h)
                go(ref, ref, s2.at[n, w, h], q2.at[n, w, h], turn[w])

    def stage3(name):
        part = parts[name]
        n = part.index
        for w in range(2):
            ref = part.out(prv if w == 0 else nxt, w)
            got(ref, s2.at[n, w, w], q2.at[n, w, w])
            go(ref, ref, s3.at[n, w], q3.at[n, w], turn[w])

    def stage4(name):
        part = parts[name]
        n = part.index
        for w in range(2):
            ref = part.out(pole, 1 - w)
            got(ref, s2.at[n, w, 1 - w], q2.at[n, w, 1 - w])
            got(ref, s3.at[n, w], q3.at[n, w])

    def m32(v):
        return pl.ds(pl.multiple_of(v, 32), 32)

    def m8(v):
        return pl.ds(pl.multiple_of(v, 8), 8)

    def m16(v):
        return pl.ds(pl.multiple_of(v, 16), 16)

    def add_rows(name, n, src, out, small=False):
        if small:
            add_part(name, n, lambda w: mids.at[n, w, pl.ds(0, 16)],
                     lambda w, h: fins.at[n, w, h, pl.ds(0, 16)], src, out)
        else:
            add_part(name, n, lambda w: mids.at[n, w], lambda w, h: fins.at[n, w, h], src, out)

    for t in range(3):
        b1, b2 = blocks(t)

        def lr_out(q, h, b1=b1, b2=b2):
            side = q // 2
            return lr.at[m32((b1 + side * (b2 - b1)) * 128 + lax.rem(q, 2) * 64 + h * 32)]

        add_rows("lr%d" % t, t, lambda q, h, t=t: ups.at[m32(FIRST[t] + q * 64 + h * 32)], lr_out)
    for t in (3, 4):
        b1 = blocks(t)[0]
        add_rows("lr%d" % t, t, lambda q, h, t=t: ups.at[m16(FIRST[t] + q * 32 + h * 16)],
                 lambda q, h, b1=b1: lr.at[m16(b1 * 128 + q * 32 + h * 16)], True)
    for j in range(2):
        add_rows("ln%d" % j, 5 + j,
                 lambda q, h, j=j: lnw.at[m32(j * 256 + q * 64 + h * 32)],
                 lambda q, h, j=j: ln.at[m32(j * 256 + q * 64 + h * 32)])
    add_rows("ld", 7, lambda q, h: low.at[m32(q * 64 + h * 32)],
             lambda q, h: ld.at[m32(q * 64 + h * 32)])
    for n, ts in ((8, slice(0, 768)), (9, slice(768, 1024))):
        add_part("of%d" % n, n, lambda w, ts=ts: omid.at[w, :, ts],
                 lambda w, h, ts=ts: ofin.at[w, h, :, ts],
                 lambda q, h, ts=ts: offd.at[m8(q * 16 + h * 8), ts],
                 lambda q, h, ts=ts: offo.at[m8(q * 16 + h * 8), ts])
    add_part("nd", 10, lambda w: gmid.at[w], lambda w, h: gfin.at[w, h],
             lambda q, h: diag.at[m8(q * 16 + h * 8)], lambda q, h: nd.at[m8(q * 16 + h * 8)])

    def lanes(q, h):
        return pl.ds(pl.multiple_of(q * 256 + h * 128, 128), 128)

    add_part("rb", 11, lambda w: rmid.at[w], lambda w, h: rfin.at[w, h],
             lambda q, h: rootw.at[:, lanes(q, h)], lambda q, h: rb.at[:, lanes(q, h)])

    def finish(p):
        w = weight[p]
        mid = jnp.transpose(mt[p]) - dn[p]
        if p == 0:
            lnw[...] = w * mid
        else:
            lnw[...] += w * mid
        ghl[:, 0:256], ghl[:, 256:512] = split(mid)

    def finish_low(p):
        low[...] -= weight[p] * three(nn, nthl[p], ghl[:, 0:256], ghl[:, 256:512])

    def offdiag_out(ts):
        for t in ts:
            for k, b in enumerate(blocks(t)):
                start = FIRST[t] + 128 * k
                no[:, pl.ds(pl.multiple_of(b * 128, 128), 128)] = offo[:, start:start + 128]

    def all_of(stage, *names):
        for name in names:
            stage(name)

    event(0, 0)
    event(0, 1)
    f_start(0)
    event(0, 2)
    event(0, 3)
    rootw[...] = weight[0] * r_ref[0] + weight[1] * r_ref[1]
    stage0("rb")
    prep_f(0)
    prep_f(1)
    loads[0].wait()
    prep_a(0)
    event(1, 0)
    f_start(1)
    prep_a(1)
    event(1, 1)
    f_relay(0)
    loads[1].wait()
    prep_n(0)
    stage1("rb")
    event(1, 2)
    prep_n(1)
    loads[2].wait()
    prep_d(0)
    event(1, 3)
    stage2("rb")
    f_last(0)
    prep_d(1)
    loads[3].wait()
    low[...] = weight[0] * lbuf[0] + weight[1] * lbuf[1]
    own_rows = pl.ds(pl.multiple_of(col * 64, 64), 64)
    diag[...] = weight[0] * dbuf[0, own_rows] + weight[1] * dbuf[1, own_rows]
    event(2, 0)
    f_relay(1)
    f_use(0)
    mate_wait(0)
    mate_wait(1)
    piece(0, 0)
    stage3("rb")
    event(2, 1)
    f_last(1)
    event(2, 2)
    f_use(1)
    event(2, 3)
    piece(0, 1)
    stage0("lr0")
    event(3, 0)
    event(3, 1)
    mate_wait(2)
    mate_wait(3)
    piece(1, 0)
    stage1("lr0")
    event(4, 0)
    event(4, 1)
    cross(5)
    cross(6)
    piece(1, 1)
    stage0("lr1")
    stage2("lr0")
    cross(7)
    mate_wait(4)
    mate_wait(5)
    piece(2, 0)
    stage1("lr1")
    stage3("lr0")
    piece(2, 1)
    all_of(stage0, "lr2", "of8")
    stage2("lr1")
    mate_wait(6)
    piece(3, 0)
    all_of(stage1, "lr2", "of8")
    piece(3, 1)
    stage0("lr3")
    stage3("lr1")
    mate_wait(7)
    piece(4, 0)
    all_of(stage2, "lr2", "of8")
    stage1("lr3")
    piece(4, 1)
    all_of(stage0, "lr4", "nd", "of9")
    finish(0)
    stage2("lr3")
    finish_low(0)
    finish(1)
    all_of(stage0, "ln0", "ln1")
    all_of(stage3, "lr2", "of8")
    all_of(stage1, "lr4", "nd", "of9")
    finish_low(1)
    stage0("ld")
    stage3("lr3")
    all_of(stage1, "ln0")
    all_of(stage2, "lr4", "nd", "of9")
    all_of(stage1, "ln1", "ld")
    all_of(stage3, "lr4", "nd", "of9")
    all_of(stage2, "ln0", "ln1", "ld")
    stage4("of8")
    offdiag_out(range(3))
    all_of(stage3, "ln0", "ln1", "ld")
    stage4("of9")
    offdiag_out(range(3, 5))
    all_of(stage4, "rb", "lr0", "lr1", "lr2", "lr3", "lr4", "nd", "ln0", "ln1", "ld")
    for copy in sent:
        copy.wait_send()


SHAPES = ((16, ROWS), (64, ROWS), (64, WIDE), (ROWS, LEAF), (WIDE, LEAF), (LEAF, LEAF))


def sweep(pattern, weights, root, factor, node_inv, leaf_root, node_leaf, leaf_inv):
    dma = pltpu.SemaphoreType.DMA
    vmem = pltpu.VMEM
    f32 = lambda *shape: vmem(shape, F32)
    bf16 = lambda *shape: vmem(shape, BF16)
    n = 12
    return pl.pallas_call(
        kernel,
        out_shape=tuple(jax.ShapeDtypeStruct(shape, F32) for shape in SHAPES),
        in_specs=[pl.BlockSpec(memory_space=pltpu.SMEM)] * 2
        + [pl.BlockSpec(memory_space=pltpu.VMEM)] * 2
        + [pl.BlockSpec(memory_space=pl.ANY)] * 4,
        out_specs=[pl.BlockSpec(memory_space=pltpu.VMEM)] * 6,
        scratch_shapes=[
            f32(2, WIDE, WIDE), f32(2, ROWS, LEAF), f32(2, WIDE, LEAF), f32(2, LEAF, LEAF),
            f32(2, Z, 128, ROWS), f32(2, WIDE, ROWS), bf16(2, 128, ROWS),
            bf16(2, WIDE + LEAF, ROWS), bf16(2, WIDE + LEAF, ROWS),
            bf16(2, WIDE, LEAF), bf16(2, WIDE, LEAF), bf16(2, 2 * LEAF, WIDE),
            f32(2, WIDE, LEAF), f32(2, LEAF, WIDE), bf16(512, ROWS), bf16(512, WIDE),
            f32(ROWS, LEAF), f32(64, ROWS), f32(64, ROWS), f32(64, WIDE), f32(16, ROWS),
            f32(WIDE, LEAF), f32(LEAF, LEAF),
            f32(8, 2, 32, LEAF), f32(8, 2, 2, 32, LEAF), f32(2, 8, ROWS), f32(2, 2, 8, ROWS),
            f32(2, 8, WIDE), f32(2, 2, 8, WIDE), f32(2, 16, 128), f32(2, 2, 16, 128),
            dma((4, 2)), dma((4, 2)), dma((2, 4, 4)), dma((2, 4, 4)), dma((8, 4)), dma((8, 4)),
            dma((3, 2)), dma((3, 2)),
            dma((2, 2)), dma((2, 2)), dma((2, 2)), dma((2, 2)), dma((2, 4)), dma((2, 4)), dma((4,)),
            dma((n, 2)), dma((n, 2)), dma((n, 2, 2)), dma((n, 2, 2)),
            dma((n, 2, 2)), dma((n, 2, 2)), dma((n, 2)), dma((n, 2)),
        ],
        compiler_params=pltpu.CompilerParams(
            collective_id=0, has_side_effects=True, vmem_limit_bytes=56 << 20
        ),
    )(pattern, weights, root, factor, node_inv, leaf_root, node_leaf, leaf_inv)


def settle_kernel(*refs):
    ins, outs, sems = refs[:6], refs[6:12], refs[12]
    copies = [pltpu.make_async_copy(a, b, sems.at[k]) for k, (a, b) in enumerate(zip(ins, outs))]
    for copy in copies:
        copy.start()
    for copy in copies:
        copy.wait()


def settle(arrays):
    return pl.pallas_call(
        settle_kernel,
        out_shape=tuple(jax.ShapeDtypeStruct(shape, F32) for shape in SHAPES),
        in_specs=[pl.BlockSpec(memory_space=pl.ANY)] * 6,
        out_specs=[pl.BlockSpec(memory_space=pl.ANY)] * 6,
        scratch_shapes=[pltpu.SemaphoreType.DMA((6,))],
    )(*arrays)


def shards(
    root_inverse,
    node_factor,
    node_inverse,
    leaf_root_factor,
    leaf_node_factor,
    leaf_inverse,
    leaf_pattern,
    pole_weight,
):
    outs = settle(sweep(
        leaf_pattern, pole_weight, root_inverse, jnp.swapaxes(node_factor[:, 0], 1, 2),
        node_inverse[:, 0], leaf_root_factor[:, 0], leaf_node_factor[:, 0], leaf_inverse[:, 0],
    ))
    return (outs[0], outs[1].T[None]) + tuple(out[None] for out in outs[2:])


def solution(mesh):
    return jax.shard_map(
        shards,
        mesh=mesh,
        in_specs=(
            P("pole", ("row", "col"), None),
            P("pole", "row", None, "col"),
            P("pole", "row", None, None),
            P("pole", ("row", "col"), None, None),
            P("pole", ("row", "col"), None, None),
            P("pole", ("row", "col"), None, None),
            P(("row", "col"), None),
            P("pole"),
        ),
        out_specs=(
            P(("row", "col"), None),
            P("row", None, "col"),
            P("row", "col", None),
            P(("row", "col"), None, None),
            P(("row", "col"), None, None),
            P(("row", "col"), None, None),
        ),
        check_vma=False,
    )
```

```python
import functools

import jax
import jax.numpy as jnp
from jax import lax
from jax.experimental import pallas as pl
from jax.experimental.pallas import tpu as pltpu
from jax.sharding import PartitionSpec as P

MESH = pl.DeviceIdType.MESH
F32, BF16 = jnp.float32, jnp.bfloat16
ROWS, WIDE, LEAF = 1024, 512, 256
Z, X = 8, 4


def split(value):
    hi = value.astype(BF16)
    return hi, (value - hi.astype(F32)).astype(BF16)


def nn(left, right):
    return lax.dot_general(left, right, (((1,), (0,)), ((), ())), preferred_element_type=F32)


def nt(left, right):
    return lax.dot_general(left, right, (((1,), (1,)), ((), ())), preferred_element_type=F32)


def three(dot, stacked, hi, lo):
    half = stacked.shape[0] // 2
    both = dot(stacked, hi)
    return both[:half] + both[half:] + dot(stacked[:half], lo)


class Part:
    def __init__(self, index, shape, mid, fin, src, out):
        self.index, self.shape, self.mid, self.fin, self.src, self.out = index, shape, mid, fin, src, out


def kernel(
    pat, weight, r_ref, ft, d_hbm, a_hbm, n_hbm, l_hbm,
    rb, no, nd, lr, ln, ld,
    dbuf, abuf, nbuf, lbuf,
    rg, fg, fhi, flo, af, qhi, qlo, nhi, nlo, nthl, dn, rs, xs, vt, vhl, mhl,
    ups, offd, offo, diag, rootw, lnw, low,
    mids, fins, omid, ofin, gmid, gfin, rmid, rfin,
    near_send, near_recv, ring_send, ring_recv, pair_send, pair_recv,
    cross_send, cross_recv, fw_send, fw_recv, fx_send, fx_recv, mate_send, mate_recv, local_sem,
    s0, q0, s1, q1, s2, q2, s3, q3,
):
    pole, row, col = lax.axis_index("pole"), lax.axis_index("row"), lax.axis_index("col")
    x, core = col // 2, lax.rem(col, 2)
    other = 1 - core

    loads = []
    for k, (src, dst) in enumerate(
        ((a_hbm, abuf), (n_hbm, nbuf), (d_hbm, dbuf), (l_hbm, lbuf))
    ):
        copy = pltpu.make_async_copy(src, dst, local_sem.at[k])
        copy.start()
        loads.append(copy)

    def at(dx, k):
        return (pole, row, lax.rem(x + dx + X, X) * 2 + k)

    along = ((pole, lax.rem(row + 1, Z), col), (pole, lax.rem(row + Z - 1, Z), col))
    beside = (at(1, core), at(X - 1, core))
    mate = (pole, row, x * 2 + other)
    nxt, prv, opp = lax.rem(pole + 1, 4), lax.rem(pole + 3, 4), lax.rem(pole + 2, 4)
    turn = ((nxt, row, col), (prv, row, col))
    owner = (nxt, prv)

    barrier = pltpu.get_barrier_semaphore()
    peers = [*along, mate, *turn] + [at(dx, k) for dx in range(1, X) for k in range(2)]
    for peer in peers:
        pl.semaphore_signal(barrier, inc=1, device_id=peer, device_id_type=MESH)
    pl.semaphore_wait(barrier, len(peers))

    def remote(src, dst, ssem, rsem, dev):
        return pltpu.make_async_remote_copy(
            src_ref=src, dst_ref=dst, send_sem=ssem, recv_sem=rsem,
            device_id=dev, device_id_type=MESH,
        )

    sent = []

    def go(src, dst, ssem, rsem, dev):
        copy = remote(src, dst, ssem, rsem, dev)
        copy.start()
        sent.append(copy)

    def got(ref, ssem, rsem):
        remote(ref, ref, ssem, rsem, mate).wait_recv()

    own = pl.ds(pl.multiple_of(col * 16, 16), 16)
    for dx in range(X):
        for flip in range(2):
            if dx or flip:
                k = other if flip else core
                go(r_ref.at[k], rg.at[k, row, own], near_send.at[dx, flip],
                   near_recv.at[(X - dx) % X, flip], at(dx, k))
    rg[core, row, own] = r_ref[core]

    def chunk(block, i):
        start = pl.multiple_of(lax.rem(x + i, X) * 32, 32)
        return rg.at[core, block, pl.ds(start, 32)]

    def to_mate(block, slot, i):
        go(chunk(block, i), chunk(block, i), pair_send.at[slot, i], pair_recv.at[slot, i], mate)

    def forward(step, i, way, block):
        if step < 2 or (step == 2 and i < 2) or (step == 3 and i == way):
            go(chunk(block, i), chunk(block, i), ring_send.at[way, step, i],
               ring_recv.at[way, step, i], along[way])

    def block_of(step, way):
        return lax.rem(row + (Z - step if way == 0 else step), Z)

    def event(step, i):
        if step == 0:
            for flip in range(2):
                if i or flip:
                    got(r_ref.at[0], near_send.at[0, 0], near_recv.at[i, flip])
            for way in range(2):
                forward(0, i, way, row)
            to_mate(row, 0, i)
            return
        for way in range(2):
            if step == 4 and i != way:
                continue
            block = block_of(step, way)
            slot = 7 if step == 4 else 1 + 2 * (step - 1) + way
            got(chunk(block, i), ring_send.at[way, step - 1, i], ring_recv.at[way, step - 1, i])
            forward(step, i, way, block)
            if step > 2:
                go(chunk(block, i), chunk(block, i), cross_send.at[slot - 5, i],
                   cross_recv.at[slot - 5, i], beside[i])
            to_mate(block, slot, i)

    def cross(slot):
        block = block_of(4 if slot == 7 else 3, (slot - 5) % 2)
        for i in range(2):
            ref = chunk(block, 3 - i)
            got(ref, cross_send.at[slot - 5, i], cross_recv.at[slot - 5, i])
            to_mate(block, slot, 3 - i)

    def mate_wait(slot):
        for i in range(4):
            got(rg.at[other, 0, pl.ds(0, 32)], pair_send.at[slot, i], pair_recv.at[slot, i])

    def frows(dx, start=0, size=64):
        first = lax.rem(x + dx, X) * 128 + core * 64 + start
        return pl.ds(pl.multiple_of(first, 32), size)

    def f_start(p):
        here = fg.at[p, frows(0)]
        for way in range(2):
            go(ft.at[p], here, fw_send.at[p, way], fw_recv.at[p, way], beside[way])
        go(ft.at[p], here, mate_send.at[p, 0], mate_recv.at[p, 0], mate)

    def f_relay(p):
        for way, dx in ((0, X - 1), (1, 1)):
            ref = fg.at[p, frows(dx)]
            got(ref, fw_send.at[p, way], fw_recv.at[p, way])
            part = fg.at[p, frows(dx, 32 * way, 32)]
            go(part, part, fx_send.at[p, way], fx_recv.at[p, way], beside[way])
            go(ref, ref, mate_send.at[p, 1 + way], mate_recv.at[p, 1 + way], mate)

    def f_last(p):
        for way in range(2):
            got(fg.at[p, frows(2, 32 * way, 32)], fx_send.at[p, way], fx_recv.at[p, way])
        ref = fg.at[p, frows(2)]
        go(ref, ref, mate_send.at[p, 3], mate_recv.at[p, 3], mate)

    def f_use(p):
        for k in range(4):
            got(ft.at[p], mate_send.at[p, k], mate_recv.at[p, k])

        def body(i, _):
            rows = pl.ds(pl.multiple_of(i * 64, 64), 64)
            fhi[p, rows], flo[p, rows] = split(fg[p, rows])
            return 0

        lax.fori_loop(0, 8, body, 0)

    def prep_f(p):
        t = ft[p]
        fg[p, frows(0)] = t
        af[p, 256:320], af[p, 576:640] = split(t)

    def prep_a(p):
        for i in range(8):
            t = jnp.transpose(abuf[p, 128 * i:128 * i + 128] * pat[0, i].astype(F32))
            cols = slice(128 * i, 128 * i + 128)
            af[p, 0:256, cols], af[p, 320:576, cols] = split(t)

    def prep_n(p):
        n = nbuf[p]
        nhi[p], nlo[p] = split(n)
        nthl[p, 0:LEAF], nthl[p, LEAF:] = split(jnp.transpose(n))

    def prep_d(p):
        for i in range(2):
            rows = slice(256 * i, 256 * i + 256)
            hi, lo = split(dbuf[p, rows])
            dn[p, rows] = nn(hi, nhi[p]) + nn(lo, nhi[p]) + nn(hi, nlo[p])

    def blocks(t):
        first = lax.rem(row + t, Z)
        return [first] if t in (0, 4) else [first, lax.rem(row + Z - t, Z)]

    FIRST = (0, 128, 384, 640, 896)

    def span(t):
        size = 128 * len(blocks(t))
        start = 2 * FIRST[t]
        return size, slice(start, start + size), slice(start + size, start + 2 * size), slice(start, start + 2 * size)

    def lane(b):
        return pl.ds(pl.multiple_of(b * 128, 128), 128)

    def pair_cols(get, t):
        cols = [get(lane(b)) for b in blocks(t)]
        return cols[0] if len(cols) == 1 else jnp.concatenate(cols, axis=1)

    def early(t, p):
        size, hi_rows, lo_rows, all_rows = span(t)
        here = slice(FIRST[t], FIRST[t] + size)
        for k, b in enumerate(blocks(t)):
            start = 2 * FIRST[t] + 128 * k
            rs[p, start:start + 128], rs[p, start + size:start + size + 128] = split(rg[p, b])
        xs[p, here] = three(nt, rs[p, all_rows], af[p, 0:256], af[p, 320:576])
        fo = jnp.concatenate([af[p, 256:320], af[p, 576:640]], axis=0)
        o = weight[p] * three(nt, fo, rs[p, hi_rows], rs[p, lo_rows])
        if p == 0:
            offd[:, here] = -o
        else:
            offd[:, here] -= o
        left = pair_cols(lambda c: af[p, :, c], t)
        for n in range(4):
            cols = slice(256 * n, 256 * n + 256)
            u = three(nn, left, rs[p, hi_rows, cols], rs[p, lo_rows, cols])
            if t == 0:
                vt[p, :, cols] = u
            else:
                vt[p, :, cols] += u

    def carry(p):
        for n in range(4):
            cols = slice(256 * n, 256 * n + 256)
            qhi[p, :, cols], qlo[p, :, cols] = split(
                three(nn, nthl[p], fhi[p, :, cols], flo[p, :, cols])
            )

    def late(t, p):
        w = weight[p]
        size, hi_rows, lo_rows, all_rows = span(t)
        here = slice(FIRST[t], FIRST[t] + size)
        y = three(nt, rs[p, all_rows], qhi[p], qlo[p])
        up = y - xs[p, here]
        if p == 0:
            ups[here] = w * up
        else:
            ups[here] += w * up
        for k, b in enumerate(blocks(t)):
            vt[p, 0:256, lane(b)] -= jnp.transpose(y[128 * k:128 * k + 128])
        at2 = jnp.concatenate(
            [pair_cols(lambda c: af[p, 0:256, c], t), pair_cols(lambda c: af[p, 320:576, c], t)], axis=0
        )
        uh, ul = split(up)
        low[...] -= w * three(nn, at2, uh, ul)

    def both(t, p):
        early(t, p)
        late(t, p)

    parts = {}

    def add_part(name, index, mid, fin, src, out):
        parts[name] = Part(index, None, mid, fin, src, out)

    def stage0(name):
        part = parts[name]
        n = part.index
        for w in range(2):
            go(part.src(opp, w), part.mid(w), s0.at[n, w], q0.at[n, w], turn[w])
        for w in range(2):
            go(part.src(owner[w], 1 - w), part.fin(w, 1 - w),
               s1.at[n, w, 1 - w], q1.at[n, w, 1 - w], turn[w])

    def stage1(name):
        part = parts[name]
        n = part.index
        for w in range(2):
            ref = part.mid(w)
            got(ref, s0.at[n, w], q0.at[n, w])
            ref[...] += part.src(owner[w], w)[...]
            go(ref, part.fin(w, w), s1.at[n, w, w], q1.at[n, w, w], turn[w])

    def stage2(name):
        part = parts[name]
        n = part.index
        for h in range(2):
            for w in range(2):
                got(part.fin(w, h), s1.at[n, w, h], q1.at[n, w, h])
            ref = part.out(pole, h)
            ref[...] = part.src(pole, h)[...] + (part.fin(0, h)[...] + part.fin(1, h)[...])
        for w in range(2):
            for h in (w, 1 - w):
                ref = part.out(pole, h)
                go(ref, ref, s2.at[n, w, h], q2.at[n, w, h], turn[w])

    def stage3(name):
        part = parts[name]
        n = part.index
        for w in range(2):
            ref = part.out(prv if w == 0 else nxt, w)
            got(ref, s2.at[n, w, w], q2.at[n, w, w])
            go(ref, ref, s3.at[n, w], q3.at[n, w], turn[w])

    def stage4(name):
        part = parts[name]
        n = part.index
        for w in range(2):
            ref = part.out(pole, 1 - w)
            got(ref, s2.at[n, w, 1 - w], q2.at[n, w, 1 - w])
            got(ref, s3.at[n, w], q3.at[n, w])

    def m32(v):
        return pl.ds(pl.multiple_of(v, 32), 32)

    def m8(v):
        return pl.ds(pl.multiple_of(v, 8), 8)

    def m16(v):
        return pl.ds(pl.multiple_of(v, 16), 16)

    def add_rows(name, n, src, out, small=False):
        if small:
            add_part(name, n, lambda w: mids.at[n, w, pl.ds(0, 16)],
                     lambda w, h: fins.at[n, w, h, pl.ds(0, 16)], src, out)
        else:
            add_part(name, n, lambda w: mids.at[n, w], lambda w, h: fins.at[n, w, h], src, out)

    for t in (1, 2, 3):
        b1, b2 = blocks(t)

        def lr_out(q, h, b1=b1, b2=b2):
            side = q // 2
            return lr.at[m32((b1 + side * (b2 - b1)) * 128 + lax.rem(q, 2) * 64 + h * 32)]

        add_rows("lr%d" % t, t, lambda q, h, t=t: ups.at[m32(FIRST[t] + q * 64 + h * 32)], lr_out)
    for t in (0, 4):
        b1 = blocks(t)[0]
        add_rows("lr%d" % t, t, lambda q, h, t=t: ups.at[m16(FIRST[t] + q * 32 + h * 16)],
                 lambda q, h, b1=b1: lr.at[m16(b1 * 128 + q * 32 + h * 16)], True)
    for j in range(2):
        add_rows("ln%d" % j, 5 + j,
                 lambda q, h, j=j: lnw.at[m32(j * 256 + q * 64 + h * 32)],
                 lambda q, h, j=j: ln.at[m32(j * 256 + q * 64 + h * 32)])
    add_rows("ld", 7, lambda q, h: low.at[m32(q * 64 + h * 32)],
             lambda q, h: ld.at[m32(q * 64 + h * 32)])
    for n, ts in ((8, slice(0, 896)), (9, slice(896, 1024))):
        add_part("of%d" % n, n, lambda w, ts=ts: omid.at[w, :, ts],
                 lambda w, h, ts=ts: ofin.at[w, h, :, ts],
                 lambda q, h, ts=ts: offd.at[m8(q * 16 + h * 8), ts],
                 lambda q, h, ts=ts: offo.at[m8(q * 16 + h * 8), ts])
    add_part("nd", 10, lambda w: gmid.at[w], lambda w, h: gfin.at[w, h],
             lambda q, h: diag.at[m8(q * 16 + h * 8)], lambda q, h: nd.at[m8(q * 16 + h * 8)])

    def lanes(q, h):
        return pl.ds(pl.multiple_of(q * 256 + h * 128, 128), 128)

    add_part("rb", 11, lambda w: rmid.at[w], lambda w, h: rfin.at[w, h],
             lambda q, h: rootw.at[:, lanes(q, h)], lambda q, h: rb.at[:, lanes(q, h)])

    def finish(p):
        w = weight[p]
        vhl[0:320], vhl[320:640] = split(vt[p])
        for n in range(2):
            rows = slice(256 * n, 256 * n + 256)
            m = three(nt, vhl[...], fhi[p, rows], flo[p, rows])
            diag[:, rows] += w * m[256:320]
            mid = jnp.transpose(m[0:256]) - dn[p, rows]
            if p == 0:
                lnw[rows] = w * mid
            else:
                lnw[rows] += w * mid
            mhl[p, rows, 0:256], mhl[p, rows, 256:512] = split(mid)

    def finish_low(p):
        low[...] -= weight[p] * three(nn, nthl[p], mhl[p, :, 0:256], mhl[p, :, 256:512])

    def offdiag_out(ts):
        for t in ts:
            for k, b in enumerate(blocks(t)):
                start = FIRST[t] + 128 * k
                no[:, pl.ds(pl.multiple_of(b * 128, 128), 128)] = offo[:, start:start + 128]

    def all_of(stage, *names):
        for name in names:
            stage(name)

    event(0, 0)
    event(0, 1)
    f_start(0)
    event(0, 2)
    event(0, 3)
    rootw[...] = weight[0] * r_ref[0] + weight[1] * r_ref[1]
    stage0("rb")
    prep_f(0)
    prep_f(1)
    loads[0].wait()
    prep_a(0)
    event(1, 0)
    prep_a(1)
    f_start(1)
    loads[1].wait()
    prep_n(0)
    prep_n(1)
    event(1, 1)
    mate_wait(0)
    early(0, 0)
    stage1("rb")
    event(1, 2)
    f_relay(0)
    early(0, 1)
    event(1, 3)
    loads[2].wait()
    prep_d(0)
    stage2("rb")
    prep_d(1)
    event(2, 0)
    loads[3].wait()
    low[...] = weight[0] * lbuf[0] + weight[1] * lbuf[1]
    own_rows = pl.ds(pl.multiple_of(col * 64, 64), 64)
    diag[...] = weight[0] * dbuf[0, own_rows] + weight[1] * dbuf[1, own_rows]
    mate_wait(1)
    mate_wait(2)
    early(1, 0)
    event(2, 1)
    f_last(0)
    early(1, 1)
    f_relay(1)
    event(2, 2)
    f_use(0)
    carry(0)
    event(2, 3)
    late(0, 0)
    late(1, 0)
    stage3("rb")
    event(3, 0)
    f_last(1)
    mate_wait(3)
    mate_wait(4)
    early(2, 0)
    event(3, 1)
    f_use(1)
    carry(1)
    late(0, 1)
    stage0("lr0")
    event(4, 0)
    event(4, 1)
    late(1, 1)
    stage0("lr1")
    early(2, 1)
    stage1("lr0")
    cross(5)
    cross(6)
    late(2, 0)
    stage1("lr1")
    stage2("lr0")
    cross(7)
    late(2, 1)
    stage0("lr2")
    stage2("lr1")
    stage3("lr0")
    mate_wait(5)
    mate_wait(6)
    both(3, 0)
    stage1("lr2")
    stage3("lr1")
    both(3, 1)
    all_of(stage0, "lr3", "of8")
    stage2("lr2")
    mate_wait(7)
    both(4, 0)
    all_of(stage1, "lr3", "of8")
    stage3("lr2")
    both(4, 1)
    all_of(stage0, "lr4", "of9")
    finish(0)
    all_of(stage2, "lr3", "of8")
    finish(1)
    all_of(stage0, "ln0", "ln1", "nd")
    finish_low(0)
    finish_low(1)
    stage0("ld")
    all_of(stage1, "lr4", "of9")
    all_of(stage3, "lr3", "of8")
    all_of(stage1, "ln0", "ln1", "nd")
    all_of(stage2, "lr4", "of9")
    stage1("ld")
    all_of(stage2, "ln0", "ln1")
    all_of(stage3, "lr4", "of9")
    all_of(stage2, "nd", "ld")
    stage4("of8")
    offdiag_out(range(4))
    all_of(stage3, "ln0", "ln1", "nd", "ld")
    stage4("of9")
    offdiag_out(range(4, 5))
    all_of(stage4, "rb", "lr0", "lr1", "lr2", "lr3", "lr4", "nd", "ln0", "ln1", "ld")
    for copy in sent:
        copy.wait_send()


SHAPES = ((16, ROWS), (64, ROWS), (64, WIDE), (ROWS, LEAF), (WIDE, LEAF), (LEAF, LEAF))


def sweep(pattern, weights, root, factor, node_inv, leaf_root, node_leaf, leaf_inv):
    dma = pltpu.SemaphoreType.DMA
    vmem = pltpu.VMEM
    f32 = lambda *shape: vmem(shape, F32)
    bf16 = lambda *shape: vmem(shape, BF16)
    n = 12
    return pl.pallas_call(
        kernel,
        out_shape=tuple(jax.ShapeDtypeStruct(shape, F32) for shape in SHAPES),
        in_specs=[pl.BlockSpec(memory_space=pltpu.SMEM)] * 2
        + [pl.BlockSpec(memory_space=pltpu.VMEM)] * 2
        + [pl.BlockSpec(memory_space=pl.ANY)] * 4,
        out_specs=[pl.BlockSpec(memory_space=pltpu.VMEM)] * 6,
        scratch_shapes=[
            f32(2, WIDE, WIDE), f32(2, ROWS, LEAF), f32(2, WIDE, LEAF), f32(2, LEAF, LEAF),
            f32(2, Z, 128, ROWS), f32(2, WIDE, ROWS),
            bf16(2, WIDE, ROWS), bf16(2, WIDE, ROWS), bf16(2, 640, ROWS),
            bf16(2, LEAF, ROWS), bf16(2, LEAF, ROWS),
            bf16(2, WIDE, LEAF), bf16(2, WIDE, LEAF), bf16(2, 2 * LEAF, WIDE),
            f32(2, WIDE, LEAF), bf16(2, 2 * ROWS, ROWS), f32(2, ROWS, LEAF), f32(2, 320, ROWS),
            bf16(640, ROWS), bf16(2, WIDE, 512),
            f32(ROWS, LEAF), f32(64, ROWS), f32(64, ROWS), f32(64, WIDE), f32(16, ROWS),
            f32(WIDE, LEAF), f32(LEAF, LEAF),
            f32(8, 2, 32, LEAF), f32(8, 2, 2, 32, LEAF), f32(2, 8, ROWS), f32(2, 2, 8, ROWS),
            f32(2, 8, WIDE), f32(2, 2, 8, WIDE), f32(2, 16, 128), f32(2, 2, 16, 128),
            dma((4, 2)), dma((4, 2)), dma((2, 4, 4)), dma((2, 4, 4)), dma((8, 4)), dma((8, 4)),
            dma((3, 2)), dma((3, 2)),
            dma((2, 2)), dma((2, 2)), dma((2, 2)), dma((2, 2)), dma((2, 4)), dma((2, 4)), dma((4,)),
            dma((n, 2)), dma((n, 2)), dma((n, 2, 2)), dma((n, 2, 2)),
            dma((n, 2, 2)), dma((n, 2, 2)), dma((n, 2)), dma((n, 2)),
        ],
        compiler_params=pltpu.CompilerParams(
            collective_id=0, has_side_effects=True, vmem_limit_bytes=56 << 20
        ),
    )(pattern, weights, root, factor, node_inv, leaf_root, node_leaf, leaf_inv)


def settle_kernel(*refs):
    ins, outs, bufs, sems = refs[:6], refs[6:12], refs[12:18], refs[18]
    down = [pltpu.make_async_copy(a, b, sems.at[0, k]) for k, (a, b) in enumerate(zip(ins, bufs))]
    up = [pltpu.make_async_copy(a, b, sems.at[1, k]) for k, (a, b) in enumerate(zip(bufs, outs))]
    for copy in down:
        copy.start()
    for first, second in zip(down, up):
        first.wait()
        second.start()
    for copy in up:
        copy.wait()


def settle(arrays):
    return pl.pallas_call(
        settle_kernel,
        out_shape=tuple(jax.ShapeDtypeStruct(shape, F32) for shape in SHAPES),
        in_specs=[pl.BlockSpec(memory_space=pl.ANY)] * 6,
        out_specs=[pl.BlockSpec(memory_space=pl.ANY)] * 6,
        scratch_shapes=[pltpu.VMEM(shape, F32) for shape in SHAPES] + [pltpu.SemaphoreType.DMA((2, 6))],
    )(*arrays)


def shards(
    root_inverse,
    node_factor,
    node_inverse,
    leaf_root_factor,
    leaf_node_factor,
    leaf_inverse,
    leaf_pattern,
    pole_weight,
):
    outs = settle(sweep(
        leaf_pattern, pole_weight, root_inverse, jnp.swapaxes(node_factor[:, 0], 1, 2),
        node_inverse[:, 0], leaf_root_factor[:, 0], leaf_node_factor[:, 0], leaf_inverse[:, 0],
    ))
    return (outs[0], outs[1].T[None]) + tuple(out[None] for out in outs[2:])


def solution(mesh):
    return jax.shard_map(
        shards,
        mesh=mesh,
        in_specs=(
            P("pole", ("row", "col"), None),
            P("pole", "row", None, "col"),
            P("pole", "row", None, None),
            P("pole", ("row", "col"), None, None),
            P("pole", ("row", "col"), None, None),
            P("pole", ("row", "col"), None, None),
            P(("row", "col"), None),
            P("pole"),
        ),
        out_specs=(
            P(("row", "col"), None),
            P("row", None, "col"),
            P("row", "col", None),
            P(("row", "col"), None, None),
            P(("row", "col"), None, None),
            P(("row", "col"), None, None),
        ),
        check_vma=False,
    )
```

```python
import functools

import jax
import jax.numpy as jnp
from jax import lax
from jax.experimental import pallas as pl
from jax.experimental.pallas import tpu as pltpu
from jax.sharding import PartitionSpec as P

MESH = pl.DeviceIdType.MESH
F32, BF16 = jnp.float32, jnp.bfloat16
ROWS, WIDE, LEAF = 1024, 512, 256
Z, X = 8, 4


def split(value):
    hi = value.astype(BF16)
    return hi, (value - hi.astype(F32)).astype(BF16)


def nn(left, right):
    return lax.dot_general(left, right, (((1,), (0,)), ((), ())), preferred_element_type=F32)


def nt(left, right):
    return lax.dot_general(left, right, (((1,), (1,)), ((), ())), preferred_element_type=F32)


def three(dot, stacked, hi, lo):
    half = stacked.shape[0] // 2
    both = dot(stacked, hi)
    return both[:half] + both[half:] + dot(stacked[:half], lo)


class Part:
    def __init__(self, index, shape, mid, fin, src, out):
        self.index, self.shape, self.mid, self.fin, self.src, self.out = index, shape, mid, fin, src, out


def kernel(
    pat, weight, r_ref, ft, d_hbm, a_hbm, n_hbm, l_hbm,
    rb, no, nd, lr, ln, ld,
    dbuf, abuf, nbuf, lbuf,
    rg, fg, fhi, flo, af, qhi, qlo, nhi, nlo, nthl, dn, rs, xs, vt, vhl, mhl,
    ups, offd, offo, diag, rootw, lnw, low,
    mids, fins, omid, ofin, gmid, gfin, rmid, rfin,
    near_send, near_recv, ring_send, ring_recv, pair_send, pair_recv,
    cross_send, cross_recv, fw_send, fw_recv, fx_send, fx_recv, mate_send, mate_recv, local_sem,
    s0, q0, s1, q1, s2, q2, s3, q3,
):
    pole, row, col = lax.axis_index("pole"), lax.axis_index("row"), lax.axis_index("col")
    x, core = col // 2, lax.rem(col, 2)
    other = 1 - core

    loads = []
    for k, (src, dst) in enumerate(
        ((a_hbm, abuf), (n_hbm, nbuf), (d_hbm, dbuf), (l_hbm, lbuf))
    ):
        copy = pltpu.make_async_copy(src, dst, local_sem.at[k])
        copy.start()
        loads.append(copy)

    def at(dx, k):
        return (pole, row, lax.rem(x + dx + X, X) * 2 + k)

    along = ((pole, lax.rem(row + 1, Z), col), (pole, lax.rem(row + Z - 1, Z), col))
    beside = (at(1, core), at(X - 1, core))
    mate = (pole, row, x * 2 + other)
    nxt, prv, opp = lax.rem(pole + 1, 4), lax.rem(pole + 3, 4), lax.rem(pole + 2, 4)
    turn = ((nxt, row, col), (prv, row, col))
    owner = (nxt, prv)

    barrier = pltpu.get_barrier_semaphore()
    peers = [*along, mate, *turn] + [at(dx, k) for dx in range(1, X) for k in range(2)]
    for peer in peers:
        pl.semaphore_signal(barrier, inc=1, device_id=peer, device_id_type=MESH)
    pl.semaphore_wait(barrier, len(peers))

    def remote(src, dst, ssem, rsem, dev):
        return pltpu.make_async_remote_copy(
            src_ref=src, dst_ref=dst, send_sem=ssem, recv_sem=rsem,
            device_id=dev, device_id_type=MESH,
        )

    sent = []

    def go(src, dst, ssem, rsem, dev):
        copy = remote(src, dst, ssem, rsem, dev)
        copy.start()
        sent.append(copy)

    def got(ref, ssem, rsem):
        remote(ref, ref, ssem, rsem, mate).wait_recv()

    own = pl.ds(pl.multiple_of(col * 16, 16), 16)
    for dx in range(X):
        for flip in range(2):
            if dx or flip:
                k = other if flip else core
                go(r_ref.at[k], rg.at[k, row, own], near_send.at[dx, flip],
                   near_recv.at[(X - dx) % X, flip], at(dx, k))
    rg[core, row, own] = r_ref[core]

    def chunk(block, i):
        start = pl.multiple_of(lax.rem(x + i, X) * 32, 32)
        return rg.at[core, block, pl.ds(start, 32)]

    def to_mate(block, slot, i):
        go(chunk(block, i), chunk(block, i), pair_send.at[slot, i], pair_recv.at[slot, i], mate)

    def forward(step, i, way, block):
        if step < 2 or (step == 2 and i < 2) or (step == 3 and i == way):
            go(chunk(block, i), chunk(block, i), ring_send.at[way, step, i],
               ring_recv.at[way, step, i], along[way])

    def block_of(step, way):
        return lax.rem(row + (Z - step if way == 0 else step), Z)

    def event(step, i):
        if step == 0:
            for flip in range(2):
                if i or flip:
                    got(r_ref.at[0], near_send.at[0, 0], near_recv.at[i, flip])
            for way in range(2):
                forward(0, i, way, row)
            to_mate(row, 0, i)
            return
        for way in range(2):
            if step == 4 and i != way:
                continue
            block = block_of(step, way)
            slot = 7 if step == 4 else 1 + 2 * (step - 1) + way
            got(chunk(block, i), ring_send.at[way, step - 1, i], ring_recv.at[way, step - 1, i])
            forward(step, i, way, block)
            if step > 2:
                go(chunk(block, i), chunk(block, i), cross_send.at[slot - 5, i],
                   cross_recv.at[slot - 5, i], beside[i])
            to_mate(block, slot, i)

    def cross(slot):
        block = block_of(4 if slot == 7 else 3, (slot - 5) % 2)
        for i in range(2):
            ref = chunk(block, 3 - i)
            got(ref, cross_send.at[slot - 5, i], cross_recv.at[slot - 5, i])
            to_mate(block, slot, 3 - i)

    def mate_wait(slot):
        for i in range(4):
            got(rg.at[other, 0, pl.ds(0, 32)], pair_send.at[slot, i], pair_recv.at[slot, i])

    def frows(dx, start=0, size=64):
        first = lax.rem(x + dx, X) * 128 + core * 64 + start
        return pl.ds(pl.multiple_of(first, 32), size)

    def f_start(p):
        here = fg.at[p, frows(0)]
        for way in range(2):
            go(ft.at[p], here, fw_send.at[p, way], fw_recv.at[p, way], beside[way])
        go(ft.at[p], here, mate_send.at[p, 0], mate_recv.at[p, 0], mate)

    def f_relay(p):
        for way, dx in ((0, X - 1), (1, 1)):
            ref = fg.at[p, frows(dx)]
            got(ref, fw_send.at[p, way], fw_recv.at[p, way])
            part = fg.at[p, frows(dx, 32 * way, 32)]
            go(part, part, fx_send.at[p, way], fx_recv.at[p, way], beside[way])
            go(ref, ref, mate_send.at[p, 1 + way], mate_recv.at[p, 1 + way], mate)

    def f_last(p):
        for way in range(2):
            got(fg.at[p, frows(2, 32 * way, 32)], fx_send.at[p, way], fx_recv.at[p, way])
        ref = fg.at[p, frows(2)]
        go(ref, ref, mate_send.at[p, 3], mate_recv.at[p, 3], mate)

    def f_use(p):
        for k in range(4):
            got(ft.at[p], mate_send.at[p, k], mate_recv.at[p, k])

        def body(i, _):
            rows = pl.ds(pl.multiple_of(i * 64, 64), 64)
            fhi[p, rows], flo[p, rows] = split(fg[p, rows])
            return 0

        lax.fori_loop(0, 8, body, 0)

    def prep_f(p):
        t = ft[p]
        fg[p, frows(0)] = t
        af[p, 256:320], af[p, 576:640] = split(t)

    def prep_a(p):
        for i in range(8):
            t = jnp.transpose(abuf[p, 128 * i:128 * i + 128] * pat[0, i].astype(F32))
            cols = slice(128 * i, 128 * i + 128)
            af[p, 0:256, cols], af[p, 320:576, cols] = split(t)

    def prep_n(p):
        n = nbuf[p]
        nhi[p], nlo[p] = split(n)
        nthl[p, 0:LEAF], nthl[p, LEAF:] = split(jnp.transpose(n))

    def prep_d(p):
        for i in range(2):
            rows = slice(256 * i, 256 * i + 256)
            hi, lo = split(dbuf[p, rows])
            dn[p, rows] = nn(hi, nhi[p]) + nn(lo, nhi[p]) + nn(hi, nlo[p])

    def blocks(t):
        first = lax.rem(row + t, Z)
        return [first] if t in (0, 4) else [first, lax.rem(row + Z - t, Z)]

    FIRST = (0, 128, 384, 640, 896)

    def span(t):
        size = 128 * len(blocks(t))
        start = 2 * FIRST[t]
        return size, slice(start, start + size), slice(start + size, start + 2 * size), slice(start, start + 2 * size)

    def lane(b):
        return pl.ds(pl.multiple_of(b * 128, 128), 128)

    def pair_cols(get, t):
        cols = [get(lane(b)) for b in blocks(t)]
        return cols[0] if len(cols) == 1 else jnp.concatenate(cols, axis=1)

    def early(t, p, first):
        size, hi_rows, lo_rows, all_rows = span(t)
        here = slice(FIRST[t], FIRST[t] + size)
        for k, b in enumerate(blocks(t)):
            start = 2 * FIRST[t] + 128 * k
            rs[p, start:start + 128], rs[p, start + size:start + size + 128] = split(rg[p, b])
        xs[p, here] = three(nt, rs[p, all_rows], af[p, 0:256], af[p, 320:576])
        fo = jnp.concatenate([af[p, 256:320], af[p, 576:640]], axis=0)
        o = weight[p] * three(nt, fo, rs[p, hi_rows], rs[p, lo_rows])
        if first:
            offd[:, here] = -o
        else:
            offd[:, here] -= o
        left = pair_cols(lambda c: af[p, :, c], t)
        for n in range(4):
            cols = slice(256 * n, 256 * n + 256)
            u = three(nn, left, rs[p, hi_rows, cols], rs[p, lo_rows, cols])
            if t == 0:
                vt[p, :, cols] = u
            else:
                vt[p, :, cols] += u

    def carry(p):
        for n in range(4):
            cols = slice(256 * n, 256 * n + 256)
            qhi[p, :, cols], qlo[p, :, cols] = split(
                three(nn, nthl[p], fhi[p, :, cols], flo[p, :, cols])
            )

    def late(t, p, first):
        w = weight[p]
        size, hi_rows, lo_rows, all_rows = span(t)
        here = slice(FIRST[t], FIRST[t] + size)
        y = three(nt, rs[p, all_rows], qhi[p], qlo[p])
        up = y - xs[p, here]
        if first:
            ups[here] = w * up
        else:
            ups[here] += w * up
        for k, b in enumerate(blocks(t)):
            vt[p, 0:256, lane(b)] -= jnp.transpose(y[128 * k:128 * k + 128])
        at2 = jnp.concatenate(
            [pair_cols(lambda c: af[p, 0:256, c], t), pair_cols(lambda c: af[p, 320:576, c], t)], axis=0
        )
        uh, ul = split(up)
        low[...] -= w * three(nn, at2, uh, ul)

    def both(t, p, first):
        early(t, p, first)
        late(t, p, first)

    parts = {}

    def add_part(name, index, mid, fin, src, out):
        parts[name] = Part(index, None, mid, fin, src, out)

    def stage0(name):
        part = parts[name]
        n = part.index
        for w in range(2):
            go(part.src(opp, w), part.mid(w), s0.at[n, w], q0.at[n, w], turn[w])
        for w in range(2):
            go(part.src(owner[w], 1 - w), part.fin(w, 1 - w),
               s1.at[n, w, 1 - w], q1.at[n, w, 1 - w], turn[w])

    def stage1(name):
        part = parts[name]
        n = part.index
        for w in range(2):
            ref = part.mid(w)
            got(ref, s0.at[n, w], q0.at[n, w])
            ref[...] += part.src(owner[w], w)[...]
            go(ref, part.fin(w, w), s1.at[n, w, w], q1.at[n, w, w], turn[w])

    def stage2(name):
        part = parts[name]
        n = part.index
        for h in range(2):
            for w in range(2):
                got(part.fin(w, h), s1.at[n, w, h], q1.at[n, w, h])
            ref = part.out(pole, h)
            ref[...] = part.src(pole, h)[...] + (part.fin(0, h)[...] + part.fin(1, h)[...])
        for w in range(2):
            for h in (w, 1 - w):
                ref = part.out(pole, h)
                go(ref, ref, s2.at[n, w, h], q2.at[n, w, h], turn[w])

    def stage3(name):
        part = parts[name]
        n = part.index
        for w in range(2):
            ref = part.out(prv if w == 0 else nxt, w)
            got(ref, s2.at[n, w, w], q2.at[n, w, w])
            go(ref, ref, s3.at[n, w], q3.at[n, w], turn[w])

    def stage4(name):
        part = parts[name]
        n = part.index
        for w in range(2):
            ref = part.out(pole, 1 - w)
            got(ref, s2.at[n, w, 1 - w], q2.at[n, w, 1 - w])
            got(ref, s3.at[n, w], q3.at[n, w])

    def m32(v):
        return pl.ds(pl.multiple_of(v, 32), 32)

    def m8(v):
        return pl.ds(pl.multiple_of(v, 8), 8)

    def m16(v):
        return pl.ds(pl.multiple_of(v, 16), 16)

    def add_rows(name, n, src, out, small=False):
        if small:
            add_part(name, n, lambda w: mids.at[n, w, pl.ds(0, 16)],
                     lambda w, h: fins.at[n, w, h, pl.ds(0, 16)], src, out)
        else:
            add_part(name, n, lambda w: mids.at[n, w], lambda w, h: fins.at[n, w, h], src, out)

    for t in (1, 2, 3):
        b1, b2 = blocks(t)

        def lr_out(q, h, b1=b1, b2=b2):
            side = q // 2
            return lr.at[m32((b1 + side * (b2 - b1)) * 128 + lax.rem(q, 2) * 64 + h * 32)]

        add_rows("lr%d" % t, t, lambda q, h, t=t: ups.at[m32(FIRST[t] + q * 64 + h * 32)], lr_out)
    for t in (0, 4):
        b1 = blocks(t)[0]
        add_rows("lr%d" % t, t, lambda q, h, t=t: ups.at[m16(FIRST[t] + q * 32 + h * 16)],
                 lambda q, h, b1=b1: lr.at[m16(b1 * 128 + q * 32 + h * 16)], True)
    for j in range(2):
        add_rows("ln%d" % j, 5 + j,
                 lambda q, h, j=j: lnw.at[m32(j * 256 + q * 64 + h * 32)],
                 lambda q, h, j=j: ln.at[m32(j * 256 + q * 64 + h * 32)])
    add_rows("ld", 7, lambda q, h: low.at[m32(q * 64 + h * 32)],
             lambda q, h: ld.at[m32(q * 64 + h * 32)])
    for n, ts in ((8, slice(0, 896)), (9, slice(896, 1024))):
        add_part("of%d" % n, n, lambda w, ts=ts: omid.at[w, :, ts],
                 lambda w, h, ts=ts: ofin.at[w, h, :, ts],
                 lambda q, h, ts=ts: offd.at[m8(q * 16 + h * 8), ts],
                 lambda q, h, ts=ts: offo.at[m8(q * 16 + h * 8), ts])
    add_part("nd", 10, lambda w: gmid.at[w], lambda w, h: gfin.at[w, h],
             lambda q, h: diag.at[m8(q * 16 + h * 8)], lambda q, h: nd.at[m8(q * 16 + h * 8)])

    def lanes(q, h):
        return pl.ds(pl.multiple_of(q * 256 + h * 128, 128), 128)

    add_part("rb", 11, lambda w: rmid.at[w], lambda w, h: rfin.at[w, h],
             lambda q, h: rootw.at[:, lanes(q, h)], lambda q, h: rb.at[:, lanes(q, h)])

    def close(p):
        vhl[p, 0:320], vhl[p, 320:640] = split(vt[p])

    def finish(n):
        rows = slice(256 * n, 256 * n + 256)
        for p in range(2):
            w = weight[p]
            m = three(nt, vhl[p], fhi[p, rows], flo[p, rows])
            diag[:, rows] += w * m[256:320]
            mid = jnp.transpose(m[0:256]) - dn[p, rows]
            if p == 0:
                lnw[rows] = w * mid
            else:
                lnw[rows] += w * mid
            mhl[p, rows, 0:256], mhl[p, rows, 256:512] = split(mid)

    def finish_low(p):
        low[...] -= weight[p] * three(nn, nthl[p], mhl[p, :, 0:256], mhl[p, :, 256:512])

    def offdiag_out(ts):
        for t in ts:
            for k, b in enumerate(blocks(t)):
                start = FIRST[t] + 128 * k
                no[:, pl.ds(pl.multiple_of(b * 128, 128), 128)] = offo[:, start:start + 128]

    def all_of(stage, *names):
        for name in names:
            stage(name)

    event(0, 0)
    event(0, 1)
    f_start(0)
    event(0, 2)
    event(0, 3)
    rootw[...] = weight[0] * r_ref[0] + weight[1] * r_ref[1]
    stage0("rb")
    prep_f(0)
    prep_f(1)
    loads[0].wait()
    prep_a(0)
    event(1, 0)
    prep_a(1)
    f_start(1)
    loads[1].wait()
    prep_n(0)
    prep_n(1)
    event(1, 1)
    mate_wait(0)
    early(0, 0, True)
    stage1("rb")
    event(1, 2)
    f_relay(0)
    early(0, 1, False)
    event(1, 3)
    loads[2].wait()
    prep_d(0)
    stage2("rb")
    prep_d(1)
    event(2, 0)
    loads[3].wait()
    low[...] = weight[0] * lbuf[0] + weight[1] * lbuf[1]
    own_rows = pl.ds(pl.multiple_of(col * 64, 64), 64)
    diag[...] = weight[0] * dbuf[0, own_rows] + weight[1] * dbuf[1, own_rows]
    mate_wait(1)
    mate_wait(2)
    early(1, 0, True)
    event(2, 1)
    f_last(0)
    early(1, 1, False)
    f_relay(1)
    event(2, 2)
    f_use(0)
    carry(0)
    event(2, 3)
    late(0, 0, True)
    late(1, 0, True)
    stage3("rb")
    event(3, 0)
    f_last(1)
    mate_wait(3)
    mate_wait(4)
    early(2, 0, True)
    event(3, 1)
    f_use(1)
    carry(1)
    late(0, 1, False)
    stage0("lr0")
    event(4, 0)
    event(4, 1)
    early(2, 1, False)
    late(1, 1, False)
    stage0("lr1")
    stage1("lr0")
    cross(5)
    cross(6)
    late(2, 0, True)
    stage1("lr1")
    stage2("lr0")
    cross(7)
    late(2, 1, False)
    stage0("lr2")
    stage2("lr1")
    stage3("lr0")
    both(3, core, True)
    stage1("lr2")
    stage3("lr1")
    mate_wait(5)
    mate_wait(6)
    both(3, other, False)
    all_of(stage0, "lr3", "of8")
    stage2("lr2")
    both(4, core, True)
    all_of(stage1, "lr3", "of8")
    stage3("lr2")
    mate_wait(7)
    both(4, other, False)
    all_of(stage0, "lr4", "of9")
    close(0)
    close(1)
    all_of(stage2, "lr3", "of8")
    finish(0)
    stage0("ln0")
    finish(1)
    all_of(stage0, "ln1", "nd")
    finish_low(0)
    finish_low(1)
    stage0("ld")
    all_of(stage1, "lr4", "of9")
    all_of(stage3, "lr3", "of8")
    all_of(stage1, "ln0", "ln1", "nd")
    all_of(stage2, "lr4", "of9")
    stage1("ld")
    all_of(stage2, "ln0", "ln1")
    all_of(stage3, "lr4", "of9")
    all_of(stage2, "nd", "ld")
    stage4("of8")
    offdiag_out(range(4))
    all_of(stage3, "ln0", "ln1", "nd", "ld")
    stage4("of9")
    offdiag_out(range(4, 5))
    all_of(stage4, "rb", "lr0", "lr1", "lr2", "lr3", "lr4", "nd", "ln0", "ln1", "ld")
    for copy in sent:
        copy.wait_send()


SHAPES = ((16, ROWS), (64, ROWS), (64, WIDE), (ROWS, LEAF), (WIDE, LEAF), (LEAF, LEAF))


def sweep(pattern, weights, root, factor, node_inv, leaf_root, node_leaf, leaf_inv):
    dma = pltpu.SemaphoreType.DMA
    vmem = pltpu.VMEM
    f32 = lambda *shape: vmem(shape, F32)
    bf16 = lambda *shape: vmem(shape, BF16)
    n = 12
    return pl.pallas_call(
        kernel,
        out_shape=tuple(pltpu.VMEM(shape, F32) for shape in SHAPES),
        in_specs=[pl.BlockSpec(memory_space=pltpu.SMEM)] * 2
        + [pl.BlockSpec(memory_space=pltpu.VMEM)] * 2
        + [pl.BlockSpec(memory_space=pl.ANY)] * 4,
        out_specs=[pl.BlockSpec(memory_space=pltpu.VMEM)] * 6,
        scratch_shapes=[
            f32(2, WIDE, WIDE), f32(2, ROWS, LEAF), f32(2, WIDE, LEAF), f32(2, LEAF, LEAF),
            f32(2, Z, 128, ROWS), f32(2, WIDE, ROWS),
            bf16(2, WIDE, ROWS), bf16(2, WIDE, ROWS), bf16(2, 640, ROWS),
            bf16(2, LEAF, ROWS), bf16(2, LEAF, ROWS),
            bf16(2, WIDE, LEAF), bf16(2, WIDE, LEAF), bf16(2, 2 * LEAF, WIDE),
            f32(2, WIDE, LEAF), bf16(2, 2 * ROWS, ROWS), f32(2, ROWS, LEAF), f32(2, 320, ROWS),
            bf16(2, 640, ROWS), bf16(2, WIDE, 512),
            f32(ROWS, LEAF), f32(64, ROWS), f32(64, ROWS), f32(64, WIDE), f32(16, ROWS),
            f32(WIDE, LEAF), f32(LEAF, LEAF),
            f32(8, 2, 32, LEAF), f32(8, 2, 2, 32, LEAF), f32(2, 8, ROWS), f32(2, 2, 8, ROWS),
            f32(2, 8, WIDE), f32(2, 2, 8, WIDE), f32(2, 16, 128), f32(2, 2, 16, 128),
            dma((4, 2)), dma((4, 2)), dma((2, 4, 4)), dma((2, 4, 4)), dma((8, 4)), dma((8, 4)),
            dma((3, 2)), dma((3, 2)),
            dma((2, 2)), dma((2, 2)), dma((2, 2)), dma((2, 2)), dma((2, 4)), dma((2, 4)), dma((4,)),
            dma((n, 2)), dma((n, 2)), dma((n, 2, 2)), dma((n, 2, 2)),
            dma((n, 2, 2)), dma((n, 2, 2)), dma((n, 2)), dma((n, 2)),
        ],
        compiler_params=pltpu.CompilerParams(
            collective_id=0, has_side_effects=True, vmem_limit_bytes=56 << 20
        ),
    )(pattern, weights, root, factor, node_inv, leaf_root, node_leaf, leaf_inv)


def settle_kernel(*refs):
    ins, outs, sems = refs[:6], refs[6:12], refs[12]
    copies = [pltpu.make_async_copy(a, b, sems.at[k]) for k, (a, b) in enumerate(zip(ins, outs))]
    for copy in copies:
        copy.start()
    for copy in copies:
        copy.wait()


def settle(arrays):
    return pl.pallas_call(
        settle_kernel,
        out_shape=tuple(jax.ShapeDtypeStruct(shape, F32) for shape in SHAPES),
        in_specs=[pl.BlockSpec(memory_space=pltpu.VMEM)] * 6,
        out_specs=[pl.BlockSpec(memory_space=pl.ANY)] * 6,
        scratch_shapes=[pltpu.SemaphoreType.DMA((6,))],
    )(*(pltpu.with_memory_space_constraint(array, pltpu.VMEM) for array in arrays))


def shards(
    root_inverse,
    node_factor,
    node_inverse,
    leaf_root_factor,
    leaf_node_factor,
    leaf_inverse,
    leaf_pattern,
    pole_weight,
):
    outs = settle(sweep(
        leaf_pattern, pole_weight, root_inverse, jnp.swapaxes(node_factor[:, 0], 1, 2),
        node_inverse[:, 0], leaf_root_factor[:, 0], leaf_node_factor[:, 0], leaf_inverse[:, 0],
    ))
    return (outs[0], outs[1].T[None]) + tuple(out[None] for out in outs[2:])


def solution(mesh):
    return jax.shard_map(
        shards,
        mesh=mesh,
        in_specs=(
            P("pole", ("row", "col"), None),
            P("pole", "row", None, "col"),
            P("pole", "row", None, None),
            P("pole", ("row", "col"), None, None),
            P("pole", ("row", "col"), None, None),
            P("pole", ("row", "col"), None, None),
            P(("row", "col"), None),
            P("pole"),
        ),
        out_specs=(
            P(("row", "col"), None),
            P("row", None, "col"),
            P("row", "col", None),
            P(("row", "col"), None, None),
            P(("row", "col"), None, None),
            P(("row", "col"), None, None),
        ),
        check_vma=False,
    )
```

```python
import functools

import jax
import jax.numpy as jnp
from jax import lax
from jax.experimental import pallas as pl
from jax.experimental.pallas import tpu as pltpu
from jax.sharding import PartitionSpec as P

MESH = pl.DeviceIdType.MESH
F32, BF16 = jnp.float32, jnp.bfloat16
ROWS, WIDE, LEAF = 1024, 512, 256
Z, X = 8, 4


def split(value):
    hi = value.astype(BF16)
    return hi, (value - hi.astype(F32)).astype(BF16)


def nn(left, right):
    return lax.dot_general(left, right, (((1,), (0,)), ((), ())), preferred_element_type=F32)


def nt(left, right):
    return lax.dot_general(left, right, (((1,), (1,)), ((), ())), preferred_element_type=F32)


def three(dot, stacked, hi, lo):
    half = stacked.shape[0] // 2
    both = dot(stacked, hi)
    return both[:half] + both[half:] + dot(stacked[:half], lo)


class Part:
    def __init__(self, index, shape, mid, fin, src, out):
        self.index, self.shape, self.mid, self.fin, self.src, self.out = index, shape, mid, fin, src, out


def kernel(
    pat, weight, r_ref, ft, d_hbm, a_hbm, n_hbm, l_hbm,
    rb, no, nd, lr, ln, ld,
    dbuf, abuf, nbuf, lbuf,
    rg, fg, fhi, flo, af, qhi, qlo, nhi, nlo, nthl, dn, rs, xs, vt, vhl, mhl,
    ups, offd, offo, diag, rootw, lnw, low,
    mids, fins, omid, ofin, gmid, gfin, rmid, rfin,
    near_send, near_recv, ring_send, ring_recv, pair_send, pair_recv,
    cross_send, cross_recv, fw_send, fw_recv, fx_send, fx_recv, mate_send, mate_recv, local_sem,
    s0, q0, s1, q1, s2, q2, s3, q3,
):
    pole, row, col = lax.axis_index("pole"), lax.axis_index("row"), lax.axis_index("col")
    x, core = col // 2, lax.rem(col, 2)
    other = 1 - core

    loads = []
    for k, (src, dst) in enumerate(
        ((a_hbm, abuf), (n_hbm, nbuf), (d_hbm, dbuf), (l_hbm, lbuf))
    ):
        copy = pltpu.make_async_copy(src, dst, local_sem.at[k])
        copy.start()
        loads.append(copy)

    def at(dx, k):
        return (pole, row, lax.rem(x + dx + X, X) * 2 + k)

    along = ((pole, lax.rem(row + 1, Z), col), (pole, lax.rem(row + Z - 1, Z), col))
    beside = (at(1, core), at(X - 1, core))
    mate = (pole, row, x * 2 + other)
    nxt, prv, opp = lax.rem(pole + 1, 4), lax.rem(pole + 3, 4), lax.rem(pole + 2, 4)
    turn = ((nxt, row, col), (prv, row, col))
    owner = (nxt, prv)

    barrier = pltpu.get_barrier_semaphore()
    peers = [*along, mate, *turn] + [at(dx, k) for dx in range(1, X) for k in range(2)]
    for peer in peers:
        pl.semaphore_signal(barrier, inc=1, device_id=peer, device_id_type=MESH)
    pl.semaphore_wait(barrier, len(peers))

    def remote(src, dst, ssem, rsem, dev):
        return pltpu.make_async_remote_copy(
            src_ref=src, dst_ref=dst, send_sem=ssem, recv_sem=rsem,
            device_id=dev, device_id_type=MESH,
        )

    sent = []

    def go(src, dst, ssem, rsem, dev):
        copy = remote(src, dst, ssem, rsem, dev)
        copy.start()
        sent.append(copy)

    def got(ref, ssem, rsem):
        remote(ref, ref, ssem, rsem, mate).wait_recv()

    own = pl.ds(pl.multiple_of(col * 16, 16), 16)
    for dx in range(X):
        for flip in range(2):
            if dx or flip:
                k = other if flip else core
                go(r_ref.at[k], rg.at[k, row, own], near_send.at[dx, flip],
                   near_recv.at[(X - dx) % X, flip], at(dx, k))
    rg[core, row, own] = r_ref[core]

    def chunk(block, i):
        start = pl.multiple_of(lax.rem(x + i, X) * 32, 32)
        return rg.at[core, block, pl.ds(start, 32)]

    def to_mate(block, slot, i):
        go(chunk(block, i), chunk(block, i), pair_send.at[slot, i], pair_recv.at[slot, i], mate)

    def forward(step, i, way, block):
        if step < 2 or (step == 2 and i < 2) or (step == 3 and i == way):
            go(chunk(block, i), chunk(block, i), ring_send.at[way, step, i],
               ring_recv.at[way, step, i], along[way])

    def block_of(step, way):
        return lax.rem(row + (Z - step if way == 0 else step), Z)

    def event(step, i):
        if step == 0:
            for flip in range(2):
                if i or flip:
                    got(r_ref.at[0], near_send.at[0, 0], near_recv.at[i, flip])
            for way in range(2):
                forward(0, i, way, row)
            to_mate(row, 0, i)
            return
        for way in range(2):
            if step == 4 and i != way:
                continue
            block = block_of(step, way)
            slot = 7 if step == 4 else 1 + 2 * (step - 1) + way
            got(chunk(block, i), ring_send.at[way, step - 1, i], ring_recv.at[way, step - 1, i])
            forward(step, i, way, block)
            if step > 2:
                go(chunk(block, i), chunk(block, i), cross_send.at[slot - 5, i],
                   cross_recv.at[slot - 5, i], beside[i])
            to_mate(block, slot, i)

    def cross(slot):
        block = block_of(4 if slot == 7 else 3, (slot - 5) % 2)
        for i in range(2):
            ref = chunk(block, 3 - i)
            got(ref, cross_send.at[slot - 5, i], cross_recv.at[slot - 5, i])
            to_mate(block, slot, 3 - i)

    def mate_wait(slot):
        for i in range(4):
            got(rg.at[other, 0, pl.ds(0, 32)], pair_send.at[slot, i], pair_recv.at[slot, i])

    def frows(dx, start=0, size=64):
        first = lax.rem(x + dx, X) * 128 + core * 64 + start
        return pl.ds(pl.multiple_of(first, 32), size)

    def f_start(p):
        here = fg.at[p, frows(0)]
        for way in range(2):
            go(ft.at[p], here, fw_send.at[p, way], fw_recv.at[p, way], beside[way])
        go(ft.at[p], here, mate_send.at[p, 0], mate_recv.at[p, 0], mate)

    def f_relay(p):
        for way, dx in ((0, X - 1), (1, 1)):
            ref = fg.at[p, frows(dx)]
            got(ref, fw_send.at[p, way], fw_recv.at[p, way])
            part = fg.at[p, frows(dx, 32 * way, 32)]
            go(part, part, fx_send.at[p, way], fx_recv.at[p, way], beside[way])
            go(ref, ref, mate_send.at[p, 1 + way], mate_recv.at[p, 1 + way], mate)

    def f_last(p):
        for way in range(2):
            got(fg.at[p, frows(2, 32 * way, 32)], fx_send.at[p, way], fx_recv.at[p, way])
        ref = fg.at[p, frows(2)]
        go(ref, ref, mate_send.at[p, 3], mate_recv.at[p, 3], mate)

    def f_use(p):
        for k in range(4):
            got(ft.at[p], mate_send.at[p, k], mate_recv.at[p, k])

        def body(i, _):
            rows = pl.ds(pl.multiple_of(i * 64, 64), 64)
            fhi[p, rows], flo[p, rows] = split(fg[p, rows])
            return 0

        lax.fori_loop(0, 8, body, 0)

    def prep_f(p):
        t = ft[p]
        fg[p, frows(0)] = t
        af[p, 256:320], af[p, 576:640] = split(t)

    def prep_a(p):
        for i in range(8):
            t = jnp.transpose(abuf[p, 128 * i:128 * i + 128] * pat[0, i].astype(F32))
            cols = slice(128 * i, 128 * i + 128)
            af[p, 0:256, cols], af[p, 320:576, cols] = split(t)

    def prep_n(p):
        n = nbuf[p]
        nhi[p], nlo[p] = split(n)
        nthl[p, 0:LEAF], nthl[p, LEAF:] = split(jnp.transpose(n))

    def prep_d(p):
        for i in range(2):
            rows = slice(256 * i, 256 * i + 256)
            hi, lo = split(dbuf[p, rows])
            dn[p, rows] = nn(hi, nhi[p]) + nn(lo, nhi[p]) + nn(hi, nlo[p])

    def blocks(t):
        first = lax.rem(row + t, Z)
        return [first] if t in (0, 4) else [first, lax.rem(row + Z - t, Z)]

    FIRST = (0, 128, 384, 640, 896)

    def span(t):
        size = 128 * len(blocks(t))
        start = 2 * FIRST[t]
        return size, slice(start, start + size), slice(start + size, start + 2 * size), slice(start, start + 2 * size)

    def lane(b):
        return pl.ds(pl.multiple_of(b * 128, 128), 128)

    def pair_cols(get, t):
        cols = [get(lane(b)) for b in blocks(t)]
        return cols[0] if len(cols) == 1 else jnp.concatenate(cols, axis=1)

    def early(t, p, first):
        size, hi_rows, lo_rows, all_rows = span(t)
        here = slice(FIRST[t], FIRST[t] + size)
        for k, b in enumerate(blocks(t)):
            start = 2 * FIRST[t] + 128 * k
            rs[p, start:start + 128], rs[p, start + size:start + size + 128] = split(rg[p, b])
        xs[p, here] = three(nt, rs[p, all_rows], af[p, 0:256], af[p, 320:576])
        fo = jnp.concatenate([af[p, 256:320], af[p, 576:640]], axis=0)
        o = weight[p] * three(nt, fo, rs[p, hi_rows], rs[p, lo_rows])
        if first:
            offd[:, here] = -o
        else:
            offd[:, here] -= o
        left = pair_cols(lambda c: af[p, :, c], t)
        for n in range(4):
            cols = slice(256 * n, 256 * n + 256)
            u = three(nn, left, rs[p, hi_rows, cols], rs[p, lo_rows, cols])
            if t == 0:
                vt[p, :, cols] = u
            else:
                vt[p, :, cols] += u

    def carry(p):
        for n in range(4):
            cols = slice(256 * n, 256 * n + 256)
            qhi[p, :, cols], qlo[p, :, cols] = split(
                three(nn, nthl[p], fhi[p, :, cols], flo[p, :, cols])
            )

    def late(t, p, first):
        w = weight[p]
        size, hi_rows, lo_rows, all_rows = span(t)
        here = slice(FIRST[t], FIRST[t] + size)
        y = three(nt, rs[p, all_rows], qhi[p], qlo[p])
        up = y - xs[p, here]
        if first:
            ups[here] = w * up
        else:
            ups[here] += w * up
        for k, b in enumerate(blocks(t)):
            vt[p, 0:256, lane(b)] -= jnp.transpose(y[128 * k:128 * k + 128])
        at2 = jnp.concatenate(
            [pair_cols(lambda c: af[p, 0:256, c], t), pair_cols(lambda c: af[p, 320:576, c], t)], axis=0
        )
        uh, ul = split(up)
        low[...] -= w * three(nn, at2, uh, ul)

    def both(t, p, first):
        early(t, p, first)
        late(t, p, first)

    parts = {}

    def add_part(name, index, mid, fin, src, out):
        parts[name] = Part(index, None, mid, fin, src, out)

    def stage0(name):
        part = parts[name]
        n = part.index
        for w in range(2):
            go(part.src(opp, w), part.mid(w), s0.at[n, w], q0.at[n, w], turn[w])
        for w in range(2):
            go(part.src(owner[w], 1 - w), part.fin(w, 1 - w),
               s1.at[n, w, 1 - w], q1.at[n, w, 1 - w], turn[w])

    def stage1(name):
        part = parts[name]
        n = part.index
        for w in range(2):
            ref = part.mid(w)
            got(ref, s0.at[n, w], q0.at[n, w])
            ref[...] += part.src(owner[w], w)[...]
            go(ref, part.fin(w, w), s1.at[n, w, w], q1.at[n, w, w], turn[w])

    def stage2(name):
        part = parts[name]
        n = part.index
        for h in range(2):
            for w in range(2):
                got(part.fin(w, h), s1.at[n, w, h], q1.at[n, w, h])
            ref = part.out(pole, h)
            ref[...] = part.src(pole, h)[...] + (part.fin(0, h)[...] + part.fin(1, h)[...])
        for w in range(2):
            for h in (w, 1 - w):
                ref = part.out(pole, h)
                go(ref, ref, s2.at[n, w, h], q2.at[n, w, h], turn[w])

    def stage3(name):
        part = parts[name]
        n = part.index
        for w in range(2):
            ref = part.out(prv if w == 0 else nxt, w)
            got(ref, s2.at[n, w, w], q2.at[n, w, w])
            go(ref, ref, s3.at[n, w], q3.at[n, w], turn[w])

    def stage4(name):
        part = parts[name]
        n = part.index
        for w in range(2):
            ref = part.out(pole, 1 - w)
            got(ref, s2.at[n, w, 1 - w], q2.at[n, w, 1 - w])
            got(ref, s3.at[n, w], q3.at[n, w])

    def m32(v):
        return pl.ds(pl.multiple_of(v, 32), 32)

    def m8(v):
        return pl.ds(pl.multiple_of(v, 8), 8)

    def m16(v):
        return pl.ds(pl.multiple_of(v, 16), 16)

    def add_rows(name, n, src, out, small=False):
        if small:
            add_part(name, n, lambda w: mids.at[n, w, pl.ds(0, 16)],
                     lambda w, h: fins.at[n, w, h, pl.ds(0, 16)], src, out)
        else:
            add_part(name, n, lambda w: mids.at[n, w], lambda w, h: fins.at[n, w, h], src, out)

    for t in (1, 2, 3):
        b1, b2 = blocks(t)

        def lr_out(q, h, b1=b1, b2=b2):
            side = q // 2
            return lr.at[m32((b1 + side * (b2 - b1)) * 128 + lax.rem(q, 2) * 64 + h * 32)]

        add_rows("lr%d" % t, t, lambda q, h, t=t: ups.at[m32(FIRST[t] + q * 64 + h * 32)], lr_out)
    for t in (0, 4):
        b1 = blocks(t)[0]
        add_rows("lr%d" % t, t, lambda q, h, t=t: ups.at[m16(FIRST[t] + q * 32 + h * 16)],
                 lambda q, h, b1=b1: lr.at[m16(b1 * 128 + q * 32 + h * 16)], True)
    for j in range(2):
        add_rows("ln%d" % j, 5 + j,
                 lambda q, h, j=j: lnw.at[m32(j * 256 + q * 64 + h * 32)],
                 lambda q, h, j=j: ln.at[m32(j * 256 + q * 64 + h * 32)])
    add_rows("ld", 7, lambda q, h: low.at[m32(q * 64 + h * 32)],
             lambda q, h: ld.at[m32(q * 64 + h * 32)])
    for n, ts in ((8, slice(0, 896)), (9, slice(896, 1024))):
        add_part("of%d" % n, n, lambda w, ts=ts: omid.at[w, :, ts],
                 lambda w, h, ts=ts: ofin.at[w, h, :, ts],
                 lambda q, h, ts=ts: offd.at[m8(q * 16 + h * 8), ts],
                 lambda q, h, ts=ts: offo.at[m8(q * 16 + h * 8), ts])
    add_part("nd", 10, lambda w: gmid.at[w], lambda w, h: gfin.at[w, h],
             lambda q, h: diag.at[m8(q * 16 + h * 8)], lambda q, h: nd.at[m8(q * 16 + h * 8)])

    def lanes(q, h):
        return pl.ds(pl.multiple_of(q * 256 + h * 128, 128), 128)

    add_part("rb", 11, lambda w: rmid.at[w], lambda w, h: rfin.at[w, h],
             lambda q, h: rootw.at[:, lanes(q, h)], lambda q, h: rb.at[:, lanes(q, h)])

    def close(p):
        vhl[p, 0:320], vhl[p, 320:640] = split(vt[p])

    def finish(n):
        rows = slice(256 * n, 256 * n + 256)
        for p in range(2):
            w = weight[p]
            m = three(nt, vhl[p], fhi[p, rows], flo[p, rows])
            diag[:, rows] += w * m[256:320]
            mid = jnp.transpose(m[0:256]) - dn[p, rows]
            if p == 0:
                lnw[rows] = w * mid
            else:
                lnw[rows] += w * mid
            mhl[p, rows, 0:256], mhl[p, rows, 256:512] = split(mid)

    def finish_low(p):
        low[...] -= weight[p] * three(nn, nthl[p], mhl[p, :, 0:256], mhl[p, :, 256:512])

    def offdiag_out(ts):
        for t in ts:
            for k, b in enumerate(blocks(t)):
                start = FIRST[t] + 128 * k
                no[:, pl.ds(pl.multiple_of(b * 128, 128), 128)] = offo[:, start:start + 128]

    def all_of(stage, *names):
        for name in names:
            stage(name)

    event(0, 0)
    event(0, 1)
    f_start(0)
    event(0, 2)
    event(0, 3)
    rootw[...] = weight[0] * r_ref[0] + weight[1] * r_ref[1]
    stage0("rb")
    prep_f(0)
    prep_f(1)
    loads[0].wait()
    prep_a(0)
    event(1, 0)
    prep_a(1)
    f_start(1)
    loads[1].wait()
    prep_n(0)
    prep_n(1)
    event(1, 1)
    mate_wait(0)
    early(0, 0, True)
    stage1("rb")
    event(1, 2)
    f_relay(0)
    early(0, 1, False)
    event(1, 3)
    loads[2].wait()
    prep_d(0)
    stage2("rb")
    prep_d(1)
    event(2, 0)
    loads[3].wait()
    low[...] = weight[0] * lbuf[0] + weight[1] * lbuf[1]
    own_rows = pl.ds(pl.multiple_of(col * 64, 64), 64)
    diag[...] = weight[0] * dbuf[0, own_rows] + weight[1] * dbuf[1, own_rows]
    mate_wait(1)
    mate_wait(2)
    early(1, 0, True)
    event(2, 1)
    f_last(0)
    early(1, 1, False)
    f_relay(1)
    event(2, 2)
    f_use(0)
    carry(0)
    event(2, 3)
    late(0, 0, True)
    late(1, 0, True)
    stage3("rb")
    event(3, 0)
    f_last(1)
    mate_wait(3)
    mate_wait(4)
    early(2, 0, True)
    event(3, 1)
    f_use(1)
    carry(1)
    late(0, 1, False)
    stage0("lr0")
    event(4, 0)
    event(4, 1)
    early(2, 1, False)
    late(1, 1, False)
    stage0("lr1")
    stage1("lr0")
    cross(5)
    cross(6)
    late(2, 0, True)
    stage1("lr1")
    stage2("lr0")
    cross(7)
    late(2, 1, False)
    stage0("lr2")
    stage2("lr1")
    stage3("lr0")
    both(3, core, True)
    stage1("lr2")
    stage3("lr1")
    mate_wait(5)
    mate_wait(6)
    both(3, other, False)
    all_of(stage0, "lr3", "of8")
    stage2("lr2")
    both(4, core, True)
    all_of(stage1, "lr3", "of8")
    stage3("lr2")
    mate_wait(7)
    both(4, other, False)
    all_of(stage0, "lr4", "of9")
    close(0)
    close(1)
    all_of(stage2, "lr3", "of8")
    finish(0)
    stage0("ln0")
    all_of(stage1, "lr4", "of9")
    finish(1)
    all_of(stage0, "ln1", "nd")
    all_of(stage3, "lr3", "of8")
    finish_low(0)
    finish_low(1)
    stage0("ld")
    all_of(stage1, "ln0", "ln1", "nd")
    all_of(stage2, "lr4", "of9")
    stage1("ld")
    all_of(stage2, "ln0", "ln1")
    all_of(stage3, "lr4", "of9")
    all_of(stage2, "nd", "ld")
    stage4("of8")
    offdiag_out(range(4))
    all_of(stage3, "ln0", "ln1", "nd", "ld")
    stage4("of9")
    offdiag_out(range(4, 5))
    all_of(stage4, "rb", "lr0", "lr1", "lr2", "lr3", "lr4", "nd", "ln0", "ln1", "ld")
    for copy in sent:
        copy.wait_send()


SHAPES = ((16, ROWS), (64, ROWS), (64, WIDE), (ROWS, LEAF), (WIDE, LEAF), (LEAF, LEAF))


def sweep(pattern, weights, root, factor, node_inv, leaf_root, node_leaf, leaf_inv):
    dma = pltpu.SemaphoreType.DMA
    vmem = pltpu.VMEM
    f32 = lambda *shape: vmem(shape, F32)
    bf16 = lambda *shape: vmem(shape, BF16)
    n = 12
    return pl.pallas_call(
        kernel,
        out_shape=tuple(pltpu.VMEM(shape, F32) for shape in SHAPES),
        in_specs=[pl.BlockSpec(memory_space=pltpu.SMEM)] * 2
        + [pl.BlockSpec(memory_space=pltpu.VMEM)] * 2
        + [pl.BlockSpec(memory_space=pl.ANY)] * 4,
        out_specs=[pl.BlockSpec(memory_space=pltpu.VMEM)] * 6,
        scratch_shapes=[
            f32(2, WIDE, WIDE), f32(2, ROWS, LEAF), f32(2, WIDE, LEAF), f32(2, LEAF, LEAF),
            f32(2, Z, 128, ROWS), f32(2, WIDE, ROWS),
            bf16(2, WIDE, ROWS), bf16(2, WIDE, ROWS), bf16(2, 640, ROWS),
            bf16(2, LEAF, ROWS), bf16(2, LEAF, ROWS),
            bf16(2, WIDE, LEAF), bf16(2, WIDE, LEAF), bf16(2, 2 * LEAF, WIDE),
            f32(2, WIDE, LEAF), bf16(2, 2 * ROWS, ROWS), f32(2, ROWS, LEAF), f32(2, 320, ROWS),
            bf16(2, 640, ROWS), bf16(2, WIDE, 512),
            f32(ROWS, LEAF), f32(64, ROWS), f32(64, ROWS), f32(64, WIDE), f32(16, ROWS),
            f32(WIDE, LEAF), f32(LEAF, LEAF),
            f32(8, 2, 32, LEAF), f32(8, 2, 2, 32, LEAF), f32(2, 8, ROWS), f32(2, 2, 8, ROWS),
            f32(2, 8, WIDE), f32(2, 2, 8, WIDE), f32(2, 16, 128), f32(2, 2, 16, 128),
            dma((4, 2)), dma((4, 2)), dma((2, 4, 4)), dma((2, 4, 4)), dma((8, 4)), dma((8, 4)),
            dma((3, 2)), dma((3, 2)),
            dma((2, 2)), dma((2, 2)), dma((2, 2)), dma((2, 2)), dma((2, 4)), dma((2, 4)), dma((4,)),
            dma((n, 2)), dma((n, 2)), dma((n, 2, 2)), dma((n, 2, 2)),
            dma((n, 2, 2)), dma((n, 2, 2)), dma((n, 2)), dma((n, 2)),
        ],
        compiler_params=pltpu.CompilerParams(
            collective_id=0, has_side_effects=True, vmem_limit_bytes=56 << 20
        ),
    )(pattern, weights, root, factor, node_inv, leaf_root, node_leaf, leaf_inv)


def settle_kernel(*refs):
    ins, outs, sems = refs[:6], refs[6:12], refs[12]
    copies = [pltpu.make_async_copy(a, b, sems.at[k]) for k, (a, b) in enumerate(zip(ins, outs))]
    for copy in copies:
        copy.start()
    for copy in copies:
        copy.wait()


def settle(arrays):
    return pl.pallas_call(
        settle_kernel,
        out_shape=tuple(jax.ShapeDtypeStruct(shape, F32) for shape in SHAPES),
        in_specs=[pl.BlockSpec(memory_space=pltpu.VMEM)] * 6,
        out_specs=[pl.BlockSpec(memory_space=pl.ANY)] * 6,
        scratch_shapes=[pltpu.SemaphoreType.DMA((6,))],
    )(*(pltpu.with_memory_space_constraint(array, pltpu.VMEM) for array in arrays))


def shards(
    root_inverse,
    node_factor,
    node_inverse,
    leaf_root_factor,
    leaf_node_factor,
    leaf_inverse,
    leaf_pattern,
    pole_weight,
):
    outs = settle(sweep(
        leaf_pattern, pole_weight, root_inverse, jnp.swapaxes(node_factor[:, 0], 1, 2),
        node_inverse[:, 0], leaf_root_factor[:, 0], leaf_node_factor[:, 0], leaf_inverse[:, 0],
    ))
    return (outs[0], outs[1].T[None]) + tuple(out[None] for out in outs[2:])


def solution(mesh):
    return jax.shard_map(
        shards,
        mesh=mesh,
        in_specs=(
            P("pole", ("row", "col"), None),
            P("pole", "row", None, "col"),
            P("pole", "row", None, None),
            P("pole", ("row", "col"), None, None),
            P("pole", ("row", "col"), None, None),
            P("pole", ("row", "col"), None, None),
            P(("row", "col"), None),
            P("pole"),
        ),
        out_specs=(
            P(("row", "col"), None),
            P("row", None, "col"),
            P("row", "col", None),
            P(("row", "col"), None, None),
            P(("row", "col"), None, None),
            P(("row", "col"), None, None),
        ),
        check_vma=False,
    )
```
